128 devices in a mesh: dp: 32 (over y, z, core), tensor: 4 (over x).
Axes of the slice: x: 4, y: 4, z: 4, core: 2. Of those that a mesh axis runs over, the one named last changes fastest.
Arguments:
- tokens: bfloat16 [16384, 4096], P('dp', 'tensor'), may hold values from -6 to 6
- grad_out: bfloat16 [16384, 4096], P('dp'), may hold values from -3 to 3
- gate_pre: bfloat16 [16384, 14336], P('dp', 'tensor'), may hold values from -9 to 9
- up_value: bfloat16 [16384, 14336], P('dp', 'tensor'), may hold values from -6 to 6
- down_weight: bfloat16 [14336, 4096], P('tensor', 'dp'), may hold values from -0.09375 to 0.09375
- in_proj: bfloat16 [128, 4096], P(None, 'tensor'), may hold values from -0.09375 to 0.09375
- out_proj: bfloat16 [128, 14336], P(None, 'tensor'), may hold values from -0.046875 to 0.046875
- test_matrix: bfloat16 [16384, 128], replicated, may hold values from -0.046875 to 0.046875
Outputs:
- factor: float32 [16384, 128], P(('dp', 'tensor'))
The draws below stay inside these ranges and needn't reach their ends.
All inputs are finite; a program needn't handle non-finite values.
Results may differ from the reference program's by a relative error of at most 0.0065.
The reference program's roundings to bfloat16 on the way (of `gate_grad`, `act_low`, `out_low`, `proj_grad` and `coeff`) count: a program that leaves them out, or rounds other values in their place, can miss the bound.
Values may be sent and summed in bfloat16 or wider, within the bound.
A program may use at most 128 MiB of HBM per device.

```python
import jax
import jax.numpy as jnp
from jax import lax

D = 4096
FF = 14336
PDIM = 128
RANK = 128
SEQ_LEN = 128
TOKENS = 16384
SEQS = 128
PROJ = 16384


def levels(rng, shape, cuts, low, high):
    gain = 1.0
    for dim, shards_of in cuts:
        heights = jax.random.uniform(jax.random.fold_in(jax.random.fold_in(rng, 6), dim), (shards_of,), jnp.float32, low / len(cuts), high / len(cuts))
        gain = gain * jnp.repeat(jnp.exp(heights), shape[dim] // shards_of).reshape((-1,) + (1,) * (len(shape) - 1 - dim))
    return gain


def noise(key, shape, deviation, bound, split=(), dtype=jnp.bfloat16):
    values = jax.random.normal(key, shape, jnp.float32) * deviation
    if len(split) > 0:
        values = levels(key, shape, split, -0.22, 0.18) * values
    return jnp.clip(values, min=-bound, max=bound).astype(dtype)


def setup_inputs(seed: int = 0) -> dict:
    key_of = jax.random.split(jax.random.key(seed), 9)
    tokens = noise(key_of[0], (TOKENS, D), 1.0, 6.0, ((0, 32), (1, 4)))
    grad_out = noise(key_of[1], (TOKENS, D), 0.5, 3.0, ((0, 32),))
    gate_pre = noise(key_of[2], (TOKENS, FF), 1.5, 9.0, ((0, 32), (1, 4)))
    up_value = noise(key_of[3], (TOKENS, FF), 1.0, 6.0, ((0, 32), (1, 4)))
    down_weight = noise(key_of[4], (FF, D), D ** -0.5, 0.09375, ((0, 4), (1, 32)))
    in_proj = noise(key_of[5], (PDIM, D), D ** -0.5, 0.09375, ((1, 4),))
    out_proj = noise(key_of[6], (PDIM, FF), FF ** -0.5, 0.046875, ((1, 4),))
    test_matrix = noise(key_of[7], (PROJ, RANK), PROJ ** -0.5, 0.046875)
    return {"tokens": tokens, "grad_out": grad_out, "gate_pre": gate_pre, "up_value": up_value, "down_weight": down_weight, "in_proj": in_proj, "out_proj": out_proj, "test_matrix": test_matrix}


def reference(tokens, grad_out, gate_pre, up_value, down_weight, in_proj, out_proj, test_matrix):
    hidden_grad = jnp.dot(grad_out.astype(jnp.float32), down_weight.T.astype(jnp.float32), preferred_element_type=jnp.float32)
    gate_wide = gate_pre.astype(jnp.float32)
    logistic = jax.nn.sigmoid(gate_wide)
    gate_grad = (hidden_grad * up_value.astype(jnp.float32) * logistic * (1.0 + gate_wide * (1.0 - logistic))).astype(jnp.bfloat16)
    act_low = jnp.dot(tokens.astype(jnp.float32), in_proj.T.astype(jnp.float32), preferred_element_type=jnp.float32).astype(jnp.bfloat16)
    out_low = jnp.dot(gate_grad.astype(jnp.float32), out_proj.T.astype(jnp.float32), preferred_element_type=jnp.float32).astype(jnp.bfloat16)
    act_seq = act_low.reshape(SEQS, SEQ_LEN, PDIM).astype(jnp.float32)
    out_seq = out_low.reshape(SEQS, SEQ_LEN, PDIM).astype(jnp.float32)
    proj_grad = jnp.einsum('slp,slq->spq', act_seq, out_seq).reshape(SEQS, PROJ).astype(jnp.bfloat16)
    coeff = jnp.dot(proj_grad.astype(jnp.float32), test_matrix.astype(jnp.float32), preferred_element_type=jnp.float32).astype(jnp.bfloat16)
    sketch = jnp.dot(proj_grad.T.astype(jnp.float32), coeff.astype(jnp.float32), preferred_element_type=jnp.float32)
    omega_wide = test_matrix.astype(jnp.float32)
    square_sum = jnp.sum(sketch * sketch)
    omega_sq = jnp.sum(omega_wide * omega_wide)
    shift = 0.1 * jnp.sqrt(square_sum / (omega_sq + 1e-06))
    shifted = sketch + shift * omega_wide
    core = jnp.dot(omega_wide.T, shifted, precision=lax.Precision.HIGHEST)
    core = 0.5 * (core + core.T)
    lower = jnp.linalg.cholesky(core)
    factor = jax.scipy.linalg.solve_triangular(lower, shifted.T, lower=True).T
    return factor
```

```python
import functools

import jax
import jax.numpy as jnp
from jax import lax
from jax.experimental import pallas as pl
from jax.experimental.pallas import tpu as pltpu
from jax.sharding import PartitionSpec as P

MESH = pl.DeviceIdType.MESH
shift_scale = 0.1
tiny_value = 1e-06

ORDER = [
    (0, 0), (3, 0), (1, 0), (0, 3), (0, 1), (2, 0), (3, 3), (3, 1),
    (1, 3), (1, 1), (0, 2), (2, 3), (2, 1), (3, 2), (1, 2), (2, 2),
]
SLOT = {home: k for k, home in enumerate(ORDER)}
ROWS = {(0, 0): (0, 512), (0, 1): (512, 512), (1, 0): (1024, 384), (1, 1): (1408, 384)}
UP, UM, VP, VM = 0, 1, 2, 3
NSEND = 60


def table(k, values):
    total = k * 0
    for j, v in enumerate(values):
        if v:
            total = total + (k == j).astype(jnp.int32) * v
    return total


def nt(a, b):
    return lax.dot_general(a, b, (((1,), (1,)), ((), ())), preferred_element_type=jnp.float32)


def tn(a, b, **kw):
    return lax.dot_general(a, b, (((0,), (0,)), ((), ())), preferred_element_type=jnp.float32, **kw)


def kernel(
    tok_h, go_h, gp_h, up_h, dw_h, ip_h, op_h, tm_h,
    y_o, a_o, gram_o, nr_o, om_o,
    w_s, g_s, gp_s, up_s, acc_s, m_s, tk_s, ip_s, op_s, tm_s,
    oacc_s, sb_s, pb_s, oa_s, xb_s, xr_s, ap_s, ar_s,
    p32_s, pr_s, cs_s, cr_s, ns_s, nr_s,
    lsem, psend, precv, ssem, rsem, sbsend, sbrecv, xsend, xrecv, asend, arecv, tsend, trecv,
):
    d = lax.axis_index("dp")
    t = lax.axis_index("tensor")
    c = lax.rem(d, 2)
    z = lax.rem(lax.div(d, 2), 4)
    y = lax.div(d, 8)
    u = y * (1 - c) + z * c
    v = z * (1 - c) + y * c
    me = d * 4 + t

    def chip(uu, vv):
        return uu * (4 - 3 * c) + vv * (1 + 3 * c)

    def mod4(a):
        return lax.rem(a + 8, 4)

    partner = (d + 1 - 2 * c, t)
    dirs = [
        (chip(mod4(u + 1), v) * 2 + c, t),
        (chip(mod4(u - 1), v) * 2 + c, t),
        (chip(u, mod4(v + 1)) * 2 + c, t),
        (chip(u, mod4(v - 1)) * 2 + c, t),
    ]
    xdev = [None] + [(d, mod4(t + j)) for j in (1, 2, 3)]

    half = pl.multiple_of(c * 1792, 256)
    other = pl.multiple_of((1 - c) * 1792, 256)
    mine = pl.ds(pl.multiple_of(c * 512, 512), 512)
    lanes = pl.ds(pl.multiple_of(c * 128, 128), 128)

    def local(i, src, dst):
        return pltpu.make_async_copy(src, dst, lsem.at[i])

    def locals_(i):
        if i == 0:
            return local(0, dw_h.at[pl.ds(half, 1024)], w_s.at[0, pl.ds(0, 1024), lanes])
        if i == 1:
            return local(1, dw_h.at[pl.ds(half + 1024, 768)], w_s.at[0, pl.ds(1024, 768), lanes])
        src, dst = [
            (go_h, g_s.at[mine]),
            (tok_h, tk_s),
            (ip_h, ip_s),
            (op_h.at[:, pl.ds(half, 1792)], op_s),
            (gp_h.at[:, pl.ds(half, 1792)], gp_s.at[mine]),
            (up_h.at[:, pl.ds(half, 1792)], up_s.at[mine]),
            (tm_h, tm_s),
        ][i - 2]
        return local(i, src, dst)

    for i in range(5):
        locals_(i).start()

    barrier = pltpu.get_barrier_semaphore()
    greeted = [partner] + dirs + xdev[1:]
    for dev in greeted:
        pl.semaphore_signal(barrier, 1, device_id=dev, device_id_type=MESH)
    pl.semaphore_wait(barrier, len(greeted))

    def remote(src, dst, ss, rs, dev):
        return pltpu.make_async_remote_copy(
            src_ref=src, dst_ref=dst, send_sem=ss, recv_sem=rs, device_id=dev, device_id_type=MESH
        )

    def partner_copies(i):
        src, dst = [
            lambda: (dw_h.at[pl.ds(other, 1024)], w_s.at[0, pl.ds(0, 1024), lanes]),
            lambda: (dw_h.at[pl.ds(other + 1024, 768)], w_s.at[0, pl.ds(1024, 768), lanes]),
            lambda: (go_h, g_s.at[mine]),
            lambda: (gp_h.at[:, pl.ds(other, 1792)], gp_s.at[mine]),
            lambda: (up_h.at[:, pl.ds(other, 1792)], up_s.at[mine]),
        ][i]()
        return remote(src, dst, psend.at[i], precv.at[i], partner)

    partner_copies(0).start()
    partner_copies(1).start()
    partner_copies(2).start()

    sends = []

    def send(dirn, src, dst, w, h):
        r0, rn = ROWS[(w, h)]
        rows = pl.ds(r0, rn)
        remote(
            w_s.at[SLOT[src], rows], w_s.at[SLOT[dst], rows],
            ssem.at[len(sends)], rsem.at[SLOT[dst], 2 * w + h], dirs[dirn],
        ).start()
        sends.append((r0, rn))

    def landed(home, w, h):
        r0, rn = ROWS[(w, h)]
        ref = w_s.at[SLOT[home], pl.ds(r0, rn)]
        remote(ref, ref, ssem.at[0], rsem.at[SLOT[home], 2 * w + h], dirs[0]).wait_recv()

    def event(home, w, h):
        du, dv = home
        landed(home, w, h)
        if dv == 0:
            if du == 3 and h == 0:
                send(UP, home, (2, 0), w, h)
            if du == 1 and h == 1:
                send(UM, home, (2, 0), w, h)
            send(VP, home, (du, 3), w, h)
            send(VM, home, (du, 1), w, h)
        elif dv == 3 and h == 0:
            send(VP, home, (du, 2), w, h)
        elif dv == 1 and h == 1:
            send(VM, home, (du, 2), w, h)

    def own_u(w):
        for k in range(2):
            send(UP, (0, 0), (3, 0), w, k)
            send(UM, (0, 0), (1, 0), w, 1 - k)

    def own_v(w):
        for k in range(2):
            send(VP, (0, 0), (0, 3), w, k)
            send(VM, (0, 0), (0, 1), w, 1 - k)

    locals_(0).wait()
    partner_copies(0).wait_recv()
    own_u(0)
    own_v(0)
    for i in range(5, 9):
        locals_(i).start()
    partner_copies(3).start()
    partner_copies(4).start()

    for n in range(7):
        acc_s[n] = jnp.zeros((1024, 256), jnp.float32)
    locals_(3).wait()
    locals_(4).wait()

    def act_part(j, carry):
        k = mod4(t + j)
        ap_s[j] = nt(tk_s[pl.ds(pl.multiple_of(k * 128, 128), 128), :], ip_s[...])
        return carry

    lax.fori_loop(0, 4, act_part, 0)

    def act_copies(j):
        return remote(ap_s.at[j], ar_s.at[j], asend.at[j], arecv.at[j], xdev[j])

    for j in (2, 1, 3):
        act_copies(j).start()

    def first_events(w):
        event((3, 0), w, 0)
        event((1, 0), w, 1)
        event((3, 0), w, 1)
        event((1, 0), w, 0)

    def pair_events(du, w):
        event((du, 3), w, 0)
        event((du, 1), w, 1)
        event((du, 3), w, 1)
        event((du, 1), w, 0)

    def both(home, w):
        event(home, w, 0)
        event(home, w, 1)

    first_events(0)
    locals_(2).wait()
    partner_copies(2).wait_recv()

    def gate(rows, n):
        cols = pl.ds(n * 256, 256)
        g = gp_s[rows, cols].astype(jnp.float32)
        s = 1.0 / (1.0 + jnp.exp(-g))
        return up_s[rows, cols].astype(jnp.float32) * s * (1.0 + g * (1.0 - s))

    def gate_first():
        def tile(i, carry):
            rows = pl.ds(pl.multiple_of(i * 128, 128), 128)
            total = jnp.zeros((128, 128), jnp.float32)
            for n in range(4):
                gg = (acc_s[n, rows, :] * gate(rows, n)).astype(jnp.bfloat16)
                total = total + nt(gg, op_s[:, n * 256 : (n + 1) * 256])
            oacc_s[i] = total
            return carry

        lax.fori_loop(0, 8, tile, 0)

    def gate_ahead():
        def tile(i, carry):
            rows = pl.ds(pl.multiple_of(i * 128, 128), 128)
            for n in range(3):
                m_s[rows, n * 256 : (n + 1) * 256] = gate(rows, n + 4)
            return carry

        lax.fori_loop(0, 8, tile, 0)

    def gram():
        def part(i, total):
            x = tm_s[pl.ds(pl.multiple_of(i * 1024, 1024), 1024), :]
            return total + tn(x, x)

        gram_o[...] = lax.fori_loop(0, 16, part, jnp.zeros((128, 128), jnp.float32))

    def at(step):
        w, k = divmod(step, 16)
        if k == 0 and w == 1:
            pass
        if k == 3:
            pair_events(0, w)
        if k == 5:
            both((2, 0), w)
            if w == 0:
                locals_(1).wait()
                partner_copies(1).wait_recv()
                own_u(1)
        if k == 6:
            pair_events(3, w)
        if k == 8:
            pair_events(1, w)
        if k == 10:
            pair_events(2, w)
            if w == 0:
                own_v(1)
            both((0, 2), w)
        if k == 13:
            both((3, 2), w)
            if w == 0:
                first_events(1)
        if k == 14:
            both((1, 2), w)
        if k == 15:
            both((2, 2), w)
        if step == 20:
            for i in range(5, 8):
                locals_(i).wait()
            partner_copies(3).wait_recv()
            partner_copies(4).wait_recv()
            gate_first()
        if step == 23:
            gate_ahead()
        if step == 25:
            locals_(8).wait()
            gram()

    def step_body(e, carry):
        for step in range(32):
            if step in (3, 5, 6, 8, 10, 13, 14, 15, 19, 20, 21, 22, 23, 24, 25, 26, 29, 30, 31):
                pl.when(e == step)(functools.partial(at, step))
        w = lax.div(e, 16)
        k = lax.rem(e, 16)
        du = table(k, [h[0] for h in ORDER])
        dv = table(k, [h[1] for h in ORDER])
        q = chip(lax.rem(u + du, 4), lax.rem(v + dv, 4))
        cols = pl.ds(pl.multiple_of(q * 256, 256), 256)

        def part(n, carry):
            m = w * 4 + n
            b = w_s[k, pl.ds(pl.multiple_of(m * 256, 256), 256), :]
            acc_s[m] += nt(g_s[:, cols], b)
            return carry

        lax.fori_loop(0, 4 - w, part, 0)
        return carry

    lax.fori_loop(0, 32, step_body, 0)

    def pb_copy(j):
        return remote(sb_s.at[j], pb_s.at[j], sbsend.at[j], sbrecv.at[j], partner)

    def x_copies(j):
        return remote(xb_s.at[j], xr_s.at[j], xsend.at[j], xrecv.at[j], xdev[j])

    def combine(j):
        pb_copy(j).wait_recv()
        xb_s[j] = oa_s[j] + pb_s[j]
        if j:
            x_copies(j).start()

    def tail(i, carry):
        j = table(lax.div(i, 2), [2, 1, 3, 0])
        own = lax.rem(i, 2)
        core = own * c + (1 - own) * (1 - c)
        k = core * 4 + lax.rem(t + j, 4)
        rows = pl.ds(pl.multiple_of(k * 128, 128), 128)
        total = oacc_s[k]
        for n in range(3):
            gg = (acc_s[n + 4, rows, :] * m_s[rows, n * 256 : (n + 1) * 256]).astype(jnp.bfloat16)
            total = total + nt(gg, op_s[:, (n + 4) * 256 : (n + 5) * 256])

        @pl.when(own == 0)
        def _():
            sb_s[j] = total
            pb_copy(j).start()

        @pl.when(own == 1)
        def _():
            oa_s[j] = total

        for step, jj in ((3, 2), (5, 1), (7, 3)):
            pl.when(i == step)(functools.partial(combine, jj))
        return carry

    lax.fori_loop(0, 8, tail, 0)
    combine(0)
    for j in (1, 2, 3):
        act_copies(j).wait_recv()
    act = (ap_s[0] + ar_s[1] + ar_s[2] + ar_s[3]).astype(jnp.bfloat16)
    for j in (1, 2, 3):
        x_copies(j).wait_recv()
    out = (xb_s[0] + xr_s[1] + xr_s[2] + xr_s[3]).astype(jnp.bfloat16)

    proj = tn(act, out).astype(jnp.bfloat16).astype(jnp.float32)
    p32_s[...] = proj[:, None, :]

    def everyone(copy_to):
        def body(r, carry):
            k = lax.rem(me + r, 128)
            copy_to(k, (lax.div(k, 4), lax.rem(k, 4))).start()
            return carry

        lax.fori_loop(1, 128, body, 0, unroll=4)

    everyone(lambda k, dev: remote(p32_s.at[k], pr_s.at[me], tsend.at[0], trecv.at[0], dev))
    pr_s[me] = p32_s[me]

    def coeff_part(i, totals):
        out = []
        for b in range(8):
            row = p32_s[i * 8 + b].astype(jnp.bfloat16)
            rows = pl.ds(pl.multiple_of(i * 1024 + b * 128, 128), 128)
            out.append(
                totals[b]
                + lax.dot_general(row, tm_s[rows, :], (((1,), (0,)), ((), ())), preferred_element_type=jnp.float32)
            )
        return tuple(out)

    totals = lax.fori_loop(0, 16, coeff_part, tuple(jnp.zeros((1, 128), jnp.float32) for _ in range(8)))
    coeff = ((totals[0] + totals[1]) + (totals[2] + totals[3])) + ((totals[4] + totals[5]) + (totals[6] + totals[7]))
    cs_s[...] = coeff
    everyone(lambda k, dev: remote(cs_s, cr_s.at[me], tsend.at[1], trecv.at[1], dev))
    cr_s[me] = coeff
    om_o[...] = tm_s[pl.ds(pl.multiple_of(me * 128, 128), 128), :].astype(jnp.float32)

    def drain(i, ref):
        return remote(ref.at[pl.ds(0, 127)], ref.at[pl.ds(0, 127)], tsend.at[i], trecv.at[i], partner)

    drain(0, pr_s).wait_recv()
    drain(1, cr_s).wait_recv()
    wide = cr_s[:, 0, :]
    narrow = wide.astype(jnp.bfloat16)
    sketch = tn(pr_s[:, 0, :].astype(jnp.bfloat16), narrow)
    squares = jnp.sum(sketch * sketch, axis=0, keepdims=True)
    ns_s[...] = squares
    everyone(lambda k, dev: remote(ns_s, nr_s.at[me], tsend.at[2], trecv.at[2], dev))
    nr_s[me] = squares
    y_o[...] = sketch
    a_o[...] = tn(wide, narrow.astype(jnp.float32), precision=lax.Precision.HIGHEST)

    for i, (r0, rn) in enumerate(sends):
        ref = w_s.at[0, pl.ds(r0, rn)]
        remote(ref, ref, ssem.at[i], rsem.at[0, 0], dirs[0]).wait_send()
    for i in range(5):
        partner_copies(i).wait_send()
    for j in (1, 2, 3):
        act_copies(j).wait_send()
        x_copies(j).wait_send()
    for j in range(4):
        pb_copy(j).wait_send()
    drain(0, pr_s).wait_send()
    drain(1, cr_s).wait_send()
    drain(2, nr_s).wait_recv()
    drain(2, nr_s).wait_send()
    nr_o[...] = jnp.sum(nr_s[:, 0, :], axis=0, keepdims=True)


def local(tokens, grad_out, gate_pre, up_value, down_weight, in_proj, out_proj, test_matrix):
    f32, bf16 = jnp.float32, jnp.bfloat16
    square = jax.ShapeDtypeStruct((128, 128), f32)
    vmem = pltpu.VMEM
    dma = pltpu.SemaphoreType.DMA
    sketch, core_sketch, gram, squares, omega_own = pl.pallas_call(
        kernel,
        out_shape=(square, square, square, jax.ShapeDtypeStruct((1, 128), f32), square),
        in_specs=[pl.BlockSpec(memory_space=pl.ANY)] * 8,
        out_specs=(pl.BlockSpec(memory_space=vmem),) * 5,
        scratch_shapes=[
            vmem((16, 1792, 256), bf16), vmem((1024, 4096), bf16), vmem((1024, 1792), bf16), vmem((1024, 1792), bf16),
            vmem((7, 1024, 256), f32), vmem((1024, 768), f32), vmem((512, 1024), bf16), vmem((128, 1024), bf16),
            vmem((128, 1792), bf16), vmem((16384, 128), bf16),
            vmem((8, 128, 128), f32), vmem((4, 128, 128), f32), vmem((4, 128, 128), f32), vmem((4, 128, 128), f32),
            vmem((4, 128, 128), f32), vmem((4, 128, 128), f32), vmem((4, 128, 128), f32), vmem((4, 128, 128), f32),
            vmem((128, 1, 128), f32), vmem((128, 1, 128), f32), vmem((1, 128), f32), vmem((128, 1, 128), f32),
            vmem((1, 128), f32), vmem((128, 1, 128), f32),
            dma((9,)), dma((5,)), dma((5,)), dma((NSEND,)), dma((16, 4)), dma((4,)), dma((4,)), dma((4,)), dma((4,)),
            dma((4,)), dma((4,)), dma((3,)), dma((3,)),
        ],
        compiler_params=pltpu.CompilerParams(
            collective_id=1, has_side_effects=True, vmem_limit_bytes=60 * 1024 * 1024
        ),
        name="gather_project_sketch",
    )(tokens, grad_out, gate_pre, up_value, down_weight, in_proj, out_proj, test_matrix)
    shift = shift_scale * jnp.sqrt(jnp.sum(squares) / (jnp.trace(gram) + tiny_value))
    core = core_sketch + shift * gram
    core = 0.5 * (core + core.T)
    lower = jnp.linalg.cholesky(core)
    shifted = sketch + shift * omega_own
    return jax.scipy.linalg.solve_triangular(lower, shifted.T, lower=True).T


def solution(mesh):
    in_specs = (
        P("dp", "tensor"),
        P("dp", None),
        P("dp", "tensor"),
        P("dp", "tensor"),
        P("tensor", "dp"),
        P(None, "tensor"),
        P(None, "tensor"),
        P(),
    )
    out_specs = P(("dp", "tensor"), None)
    return jax.shard_map(local, mesh=mesh, in_specs=in_specs, out_specs=out_specs, check_vma=False)
```

```python
import functools

import jax
import jax.numpy as jnp
from jax import lax
from jax.experimental import pallas as pl
from jax.experimental.pallas import tpu as pltpu
from jax.sharding import PartitionSpec as P

MESH = pl.DeviceIdType.MESH
shift_scale = 0.1
tiny_value = 1e-06

ORDER = [
    (0, 0), (3, 0), (1, 0), (0, 3), (0, 1), (2, 0), (3, 3), (3, 1),
    (1, 3), (1, 1), (0, 2), (2, 3), (2, 1), (3, 2), (1, 2), (2, 2),
]
SLOT = {home: k for k, home in enumerate(ORDER)}
ROWS = {(0, 0): (0, 512), (0, 1): (512, 512), (1, 0): (1024, 384), (1, 1): (1408, 384)}
UP, UM, VP, VM = 0, 1, 2, 3
NSEND = 60


def table(k, values):
    total = k * 0
    for j, v in enumerate(values):
        if v:
            total = total + (k == j).astype(jnp.int32) * v
    return total


def nt(a, b):
    return lax.dot_general(a, b, (((1,), (1,)), ((), ())), preferred_element_type=jnp.float32)


def tn(a, b, **kw):
    return lax.dot_general(a, b, (((0,), (0,)), ((), ())), preferred_element_type=jnp.float32, **kw)


def kernel(
    tok_h, go_h, gp_h, up_h, dw_h, ip_h, op_h, tm_h,
    y_o, a_o, gram_o, nr_o, sq_o, om_o,
    w_s, g_s, gp_s, up_s, acc_s, m_s, tk_s, ip_s, op_s, tm_s,
    oacc_s, sb_s, pb_s, oa_s, xb_s, xr_s, ap_s, ar_s,
    p32_s, pr_s, cs_s, cr_s, ns_s, nr_s, gram_s,
    lsem, psend, precv, ssem, rsem, sbsend, sbrecv, xsend, xrecv, asend, arecv, tsend, trecv,
):
    d = lax.axis_index("dp")
    t = lax.axis_index("tensor")
    c = lax.rem(d, 2)
    z = lax.rem(lax.div(d, 2), 4)
    y = lax.div(d, 8)
    u = y * (1 - c) + z * c
    v = z * (1 - c) + y * c
    me = d * 4 + t

    def chip(uu, vv):
        return uu * (4 - 3 * c) + vv * (1 + 3 * c)

    def mod4(a):
        return lax.rem(a + 8, 4)

    partner = (d + 1 - 2 * c, t)
    dirs = [
        (chip(mod4(u + 1), v) * 2 + c, t),
        (chip(mod4(u - 1), v) * 2 + c, t),
        (chip(u, mod4(v + 1)) * 2 + c, t),
        (chip(u, mod4(v - 1)) * 2 + c, t),
    ]
    xdev = [None] + [(d, mod4(t + j)) for j in (1, 2, 3)]

    half = pl.multiple_of(c * 1792, 256)
    other = pl.multiple_of((1 - c) * 1792, 256)
    mine = pl.ds(pl.multiple_of(c * 512, 512), 512)
    lanes = pl.ds(pl.multiple_of(c * 128, 128), 128)

    def local(i, src, dst):
        return pltpu.make_async_copy(src, dst, lsem.at[i])

    def locals_(i):
        if i == 0:
            return local(0, dw_h.at[pl.ds(half, 1024)], w_s.at[0, pl.ds(0, 1024), lanes])
        if i == 1:
            return local(1, dw_h.at[pl.ds(half + 1024, 768)], w_s.at[0, pl.ds(1024, 768), lanes])
        src, dst = [
            (go_h, g_s.at[mine]),
            (tok_h, tk_s),
            (ip_h, ip_s),
            (op_h.at[:, pl.ds(half, 1792)], op_s),
            (gp_h.at[:, pl.ds(half, 1792)], gp_s.at[mine]),
            (up_h.at[:, pl.ds(half, 1792)], up_s.at[mine]),
            (tm_h, tm_s),
        ][i - 2]
        return local(i, src, dst)

    for i in range(5):
        locals_(i).start()

    barrier = pltpu.get_barrier_semaphore()
    greeted = [partner] + dirs + xdev[1:]
    for dev in greeted:
        pl.semaphore_signal(barrier, 1, device_id=dev, device_id_type=MESH)
    pl.semaphore_wait(barrier, len(greeted))

    def remote(src, dst, ss, rs, dev):
        return pltpu.make_async_remote_copy(
            src_ref=src, dst_ref=dst, send_sem=ss, recv_sem=rs, device_id=dev, device_id_type=MESH
        )

    def partner_copies(i):
        src, dst = [
            lambda: (dw_h.at[pl.ds(other, 1024)], w_s.at[0, pl.ds(0, 1024), lanes]),
            lambda: (dw_h.at[pl.ds(other + 1024, 768)], w_s.at[0, pl.ds(1024, 768), lanes]),
            lambda: (go_h, g_s.at[mine]),
            lambda: (gp_h.at[:, pl.ds(other, 1792)], gp_s.at[mine]),
            lambda: (up_h.at[:, pl.ds(other, 1792)], up_s.at[mine]),
        ][i]()
        return remote(src, dst, psend.at[i], precv.at[i], partner)

    partner_copies(0).start()
    partner_copies(1).start()
    partner_copies(2).start()

    sends = []

    def send(dirn, src, dst, w, h):
        r0, rn = ROWS[(w, h)]
        rows = pl.ds(r0, rn)
        remote(
            w_s.at[SLOT[src], rows], w_s.at[SLOT[dst], rows],
            ssem.at[len(sends)], rsem.at[SLOT[dst], 2 * w + h], dirs[dirn],
        ).start()
        sends.append((r0, rn))

    def landed(home, w, h):
        r0, rn = ROWS[(w, h)]
        ref = w_s.at[SLOT[home], pl.ds(r0, rn)]
        remote(ref, ref, ssem.at[0], rsem.at[SLOT[home], 2 * w + h], dirs[0]).wait_recv()

    def event(home, w, h):
        du, dv = home
        landed(home, w, h)
        if dv == 0:
            if du == 3 and h == 0:
                send(UP, home, (2, 0), w, h)
            if du == 1 and h == 1:
                send(UM, home, (2, 0), w, h)
            send(VP, home, (du, 3), w, h)
            send(VM, home, (du, 1), w, h)
        elif dv == 3 and h == 0:
            send(VP, home, (du, 2), w, h)
        elif dv == 1 and h == 1:
            send(VM, home, (du, 2), w, h)

    def own_u(w):
        for k in range(2):
            send(UP, (0, 0), (3, 0), w, k)
            send(UM, (0, 0), (1, 0), w, 1 - k)

    def own_v(w):
        for k in range(2):
            send(VP, (0, 0), (0, 3), w, k)
            send(VM, (0, 0), (0, 1), w, 1 - k)

    locals_(0).wait()
    partner_copies(0).wait_recv()
    own_u(0)
    own_v(0)
    for i in range(5, 9):
        locals_(i).start()
    partner_copies(3).start()
    partner_copies(4).start()

    for n in range(7):
        acc_s[n] = jnp.zeros((1024, 256), jnp.float32)
    locals_(3).wait()
    locals_(4).wait()

    def act_part(j, carry):
        k = mod4(t + j)
        ap_s[j] = nt(tk_s[pl.ds(pl.multiple_of(k * 128, 128), 128), :], ip_s[...])
        return carry

    lax.fori_loop(0, 4, act_part, 0)

    def act_copies(j):
        return remote(ap_s.at[j], ar_s.at[j], asend.at[j], arecv.at[j], xdev[j])

    for j in (2, 1, 3):
        act_copies(j).start()

    def first_events(w):
        event((3, 0), w, 0)
        event((1, 0), w, 1)
        event((3, 0), w, 1)
        event((1, 0), w, 0)

    def pair_events(du, w):
        event((du, 3), w, 0)
        event((du, 1), w, 1)
        event((du, 3), w, 1)
        event((du, 1), w, 0)

    def both(home, w):
        event(home, w, 0)
        event(home, w, 1)

    first_events(0)
    locals_(2).wait()
    partner_copies(2).wait_recv()

    def gate(rows, n):
        cols = pl.ds(n * 256, 256)
        g = gp_s[rows, cols].astype(jnp.float32)
        s = 1.0 / (1.0 + jnp.exp(-g))
        return up_s[rows, cols].astype(jnp.float32) * s * (1.0 + g * (1.0 - s))

    def gate_first():
        def tile(i, carry):
            rows = pl.ds(pl.multiple_of(i * 128, 128), 128)
            total = jnp.zeros((128, 128), jnp.float32)
            for n in range(4):
                gg = (acc_s[n, rows, :] * gate(rows, n)).astype(jnp.bfloat16)
                total = total + nt(gg, op_s[:, n * 256 : (n + 1) * 256])
            oacc_s[i] = total
            return carry

        lax.fori_loop(0, 8, tile, 0)

    def gate_ahead():
        def tile(i, carry):
            rows = pl.ds(pl.multiple_of(i * 128, 128), 128)
            for n in range(3):
                m_s[rows, n * 256 : (n + 1) * 256] = gate(rows, n + 4)
            return carry

        lax.fori_loop(0, 8, tile, 0)

    def gram():
        def part(i, total):
            x = tm_s[pl.ds(pl.multiple_of(i * 1024, 1024), 1024), :]
            return total + tn(x, x)

        gram_s[...] = lax.fori_loop(0, 16, part, jnp.zeros((128, 128), jnp.float32))

    def at(step):
        w, k = divmod(step, 16)
        if k == 0 and w == 1:
            pass
        if k == 3:
            pair_events(0, w)
        if k == 5:
            both((2, 0), w)
            if w == 0:
                locals_(1).wait()
                partner_copies(1).wait_recv()
                own_u(1)
        if k == 6:
            pair_events(3, w)
        if k == 8:
            pair_events(1, w)
        if k == 10:
            pair_events(2, w)
            if w == 0:
                own_v(1)
            both((0, 2), w)
        if k == 13:
            both((3, 2), w)
            if w == 0:
                first_events(1)
        if k == 14:
            both((1, 2), w)
        if k == 15:
            both((2, 2), w)
        if step == 20:
            for i in range(5, 8):
                locals_(i).wait()
            partner_copies(3).wait_recv()
            partner_copies(4).wait_recv()
            gate_first()
        if step == 23:
            gate_ahead()
        if step == 25:
            locals_(8).wait()
            gram()

    def step_body(e, carry):
        for step in range(32):
            if step in (3, 5, 6, 8, 10, 13, 14, 15, 19, 20, 21, 22, 23, 24, 25, 26, 29, 30, 31):
                pl.when(e == step)(functools.partial(at, step))
        w = lax.div(e, 16)
        k = lax.rem(e, 16)
        du = table(k, [h[0] for h in ORDER])
        dv = table(k, [h[1] for h in ORDER])
        q = chip(lax.rem(u + du, 4), lax.rem(v + dv, 4))
        cols = pl.ds(pl.multiple_of(q * 256, 256), 256)

        def part(n, carry):
            m = w * 4 + n
            b = w_s[k, pl.ds(pl.multiple_of(m * 256, 256), 256), :]
            acc_s[m] += nt(g_s[:, cols], b)
            return carry

        lax.fori_loop(0, 4 - w, part, 0)
        return carry

    lax.fori_loop(0, 32, step_body, 0)

    def pb_copy(j):
        return remote(sb_s.at[j], pb_s.at[j], sbsend.at[j], sbrecv.at[j], partner)

    def x_copies(j):
        return remote(xb_s.at[j], xr_s.at[j], xsend.at[j], xrecv.at[j], xdev[j])

    def combine(j):
        pb_copy(j).wait_recv()
        xb_s[j] = oa_s[j] + pb_s[j]
        if j:
            x_copies(j).start()

    def tail(i, carry):
        j = table(lax.div(i, 2), [2, 1, 3, 0])
        own = lax.rem(i, 2)
        core = own * c + (1 - own) * (1 - c)
        k = core * 4 + lax.rem(t + j, 4)
        rows = pl.ds(pl.multiple_of(k * 128, 128), 128)
        total = oacc_s[k]
        for n in range(3):
            gg = (acc_s[n + 4, rows, :] * m_s[rows, n * 256 : (n + 1) * 256]).astype(jnp.bfloat16)
            total = total + nt(gg, op_s[:, (n + 4) * 256 : (n + 5) * 256])

        @pl.when(own == 0)
        def _():
            sb_s[j] = total
            pb_copy(j).start()

        @pl.when(own == 1)
        def _():
            oa_s[j] = total

        for step, jj in ((3, 2), (5, 1), (7, 3)):
            pl.when(i == step)(functools.partial(combine, jj))
        return carry

    lax.fori_loop(0, 8, tail, 0)
    combine(0)
    for j in (1, 2, 3):
        act_copies(j).wait_recv()
    act = (ap_s[0] + ar_s[1] + ar_s[2] + ar_s[3]).astype(jnp.bfloat16)
    for j in (1, 2, 3):
        x_copies(j).wait_recv()
    out = (xb_s[0] + xr_s[1] + xr_s[2] + xr_s[3]).astype(jnp.bfloat16)

    proj = tn(act, out).astype(jnp.bfloat16).astype(jnp.float32)
    p32_s[...] = proj[:, None, :]

    def everyone(copy_to):
        def body(r, carry):
            k = lax.rem(me + r, 128)
            copy_to(k, (lax.div(k, 4), lax.rem(k, 4))).start()
            return carry

        lax.fori_loop(1, 128, body, 0, unroll=4)

    everyone(lambda k, dev: remote(p32_s.at[k], pr_s.at[me], tsend.at[0], trecv.at[0], dev))
    pr_s[me] = p32_s[me]

    def coeff_part(i, totals):
        out = []
        for b in range(8):
            row = p32_s[i * 8 + b].astype(jnp.bfloat16)
            rows = pl.ds(pl.multiple_of(i * 1024 + b * 128, 128), 128)
            out.append(
                totals[b]
                + lax.dot_general(row, tm_s[rows, :], (((1,), (0,)), ((), ())), preferred_element_type=jnp.float32)
            )
        return tuple(out)

    totals = lax.fori_loop(0, 16, coeff_part, tuple(jnp.zeros((1, 128), jnp.float32) for _ in range(8)))
    coeff = ((totals[0] + totals[1]) + (totals[2] + totals[3])) + ((totals[4] + totals[5]) + (totals[6] + totals[7]))
    cs_s[...] = coeff
    everyone(lambda k, dev: remote(cs_s, cr_s.at[me], tsend.at[1], trecv.at[1], dev))
    cr_s[me] = coeff
    om_o[...] = tm_s[pl.ds(pl.multiple_of(me * 128, 128), 128), :].astype(jnp.float32)

    def drain(i, ref):
        return remote(ref.at[pl.ds(0, 127)], ref.at[pl.ds(0, 127)], tsend.at[i], trecv.at[i], partner)

    drain(0, pr_s).wait_recv()
    drain(1, cr_s).wait_recv()
    wide = cr_s[:, 0, :]
    narrow = wide.astype(jnp.bfloat16)
    sketch = tn(pr_s[:, 0, :].astype(jnp.bfloat16), narrow)
    squares = jnp.sum(sketch * sketch, axis=0, keepdims=True)
    ns_s[...] = squares
    everyone(lambda k, dev: remote(ns_s, nr_s.at[me], tsend.at[2], trecv.at[2], dev))
    nr_s[me] = squares
    y_o[...] = sketch
    core = tn(wide, narrow.astype(jnp.float32), precision=lax.Precision.HIGHEST)
    a_o[...] = 0.5 * (core + core.T)
    gram_all = gram_s[...]
    gram_o[...] = 0.5 * (gram_all + gram_all.T)
    eye = lax.broadcasted_iota(jnp.int32, (128, 128), 0) == lax.broadcasted_iota(jnp.int32, (128, 128), 1)
    sq_o[...] = jnp.sum(jnp.where(eye, gram_all, 0.0), axis=0, keepdims=True)

    for i, (r0, rn) in enumerate(sends):
        ref = w_s.at[0, pl.ds(r0, rn)]
        remote(ref, ref, ssem.at[i], rsem.at[0, 0], dirs[0]).wait_send()
    for i in range(5):
        partner_copies(i).wait_send()
    for j in (1, 2, 3):
        act_copies(j).wait_send()
        x_copies(j).wait_send()
    for j in range(4):
        pb_copy(j).wait_send()
    drain(0, pr_s).wait_send()
    drain(1, cr_s).wait_send()
    drain(2, nr_s).wait_recv()
    drain(2, nr_s).wait_send()
    nr_o[...] = jnp.sum(nr_s[:, 0, :], axis=0, keepdims=True)


def eliminate(groups):
    groups = list(groups)
    lane = lax.broadcasted_iota(jnp.int32, (8, 128), 1)
    sub = lax.broadcasted_iota(jnp.int32, (8, 128), 0)

    def wide(x):
        return jnp.broadcast_to(x, (8, 128))

    for g in range(16):
        k0 = 8 * g
        inside = (lane >= k0) & (lane < k0 + 8)
        block = groups[g]
        columns = [wide(block[:, k0 + b : k0 + b + 1]) for b in range(8)]
        low = [[wide(columns[b][a : a + 1, :]) if b >= a else None for b in range(8)] for a in range(8)]
        mult = [[None] * 8 for _ in range(8)]
        inv = []
        for a in range(8):
            inv.append(1.0 / low[a][a])
            for b in range(a + 1, 8):
                mult[b][a] = low[a][b] * inv[a]
            for b in range(a + 1, 8):
                for e in range(b, 8):
                    low[b][e] = low[b][e] - mult[b][a] * low[a][e]
        rows = []
        for a in range(8):
            x = jnp.where(inside, jnp.where(lane == k0 + a, 1.0, 0.0), wide(block[a : a + 1, :]))
            for b in range(a):
                x = x - mult[a][b] * rows[b]
            rows.append(x)
        done = block
        for a in range(8):
            done = jnp.where(sub == a, rows[a] * lax.rsqrt(low[a][a]), done)
        groups[g] = done
        for h in range(g + 1, 16):
            below = groups[h]
            solved = []
            for a in range(8):
                x = wide(below[:, k0 + a : k0 + a + 1])
                for b in range(a):
                    x = x - mult[a][b] * solved[b]
                solved.append(x)
            x = jnp.where(inside, 0.0, below)
            for a in range(8):
                x = x - (solved[a] * inv[a]) * rows[a]
            groups[h] = x
    return groups


def finish(y_ref, core_ref, gram_ref, nr_ref, sq_ref, om_ref, out_ref):
    square_sum = jnp.sum(nr_ref[...], axis=1, keepdims=True)
    omega_sq = jnp.sum(sq_ref[...], axis=1, keepdims=True)
    shift = shift_scale * jnp.sqrt(square_sum / (omega_sq + tiny_value))
    core = core_ref[...] + shift * gram_ref[...]
    inverse = jnp.concatenate(eliminate([core[8 * g : 8 * g + 8, :] for g in range(16)]), axis=0)
    under = lax.broadcasted_iota(jnp.int32, (128, 128), 1) <= lax.broadcasted_iota(jnp.int32, (128, 128), 0)
    inverse = jnp.where(under, inverse, 0.0)
    shifted = y_ref[...] + shift * om_ref[...]
    out_ref[...] = lax.dot_general(
        shifted, inverse, (((1,), (1,)), ((), ())),
        precision=lax.Precision.HIGHEST, preferred_element_type=jnp.float32,
    )


def local(tokens, grad_out, gate_pre, up_value, down_weight, in_proj, out_proj, test_matrix):
    f32, bf16 = jnp.float32, jnp.bfloat16
    square = jax.ShapeDtypeStruct((128, 128), f32)
    vmem = pltpu.VMEM
    dma = pltpu.SemaphoreType.DMA
    row = jax.ShapeDtypeStruct((1, 128), f32)
    sketch, core_sketch, gram, squares, omega_sq, omega_own = pl.pallas_call(
        kernel,
        out_shape=(square, square, square, row, row, square),
        in_specs=[pl.BlockSpec(memory_space=pl.ANY)] * 8,
        out_specs=(pl.BlockSpec(memory_space=vmem),) * 6,
        scratch_shapes=[
            vmem((16, 1792, 256), bf16), vmem((1024, 4096), bf16), vmem((1024, 1792), bf16), vmem((1024, 1792), bf16),
            vmem((7, 1024, 256), f32), vmem((1024, 768), f32), vmem((512, 1024), bf16), vmem((128, 1024), bf16),
            vmem((128, 1792), bf16), vmem((16384, 128), bf16),
            vmem((8, 128, 128), f32), vmem((4, 128, 128), f32), vmem((4, 128, 128), f32), vmem((4, 128, 128), f32),
            vmem((4, 128, 128), f32), vmem((4, 128, 128), f32), vmem((4, 128, 128), f32), vmem((4, 128, 128), f32),
            vmem((128, 1, 128), f32), vmem((128, 1, 128), f32), vmem((1, 128), f32), vmem((128, 1, 128), f32),
            vmem((1, 128), f32), vmem((128, 1, 128), f32), vmem((128, 128), f32),
            dma((9,)), dma((5,)), dma((5,)), dma((NSEND,)), dma((16, 4)), dma((4,)), dma((4,)), dma((4,)), dma((4,)),
            dma((4,)), dma((4,)), dma((3,)), dma((3,)),
        ],
        compiler_params=pltpu.CompilerParams(
            collective_id=1, has_side_effects=True, vmem_limit_bytes=60 * 1024 * 1024
        ),
        name="gather_project_sketch",
    )(tokens, grad_out, gate_pre, up_value, down_weight, in_proj, out_proj, test_matrix)
    return pl.pallas_call(
        finish,
        out_shape=square,
        in_specs=[pl.BlockSpec(memory_space=vmem)] * 6,
        out_specs=pl.BlockSpec(memory_space=vmem),
        name="factor",
    )(sketch, core_sketch, gram, squares, omega_sq, omega_own)


def solution(mesh):
    in_specs = (
        P("dp", "tensor"),
        P("dp", None),
        P("dp", "tensor"),
        P("dp", "tensor"),
        P("tensor", "dp"),
        P(None, "tensor"),
        P(None, "tensor"),
        P(),
    )
    out_specs = P(("dp", "tensor"), None)
    return jax.shard_map(local, mesh=mesh, in_specs=in_specs, out_specs=out_specs, check_vma=False)
```

```python
import functools

import jax
import jax.numpy as jnp
from jax import lax
from jax.experimental import pallas as pl
from jax.experimental.pallas import tpu as pltpu
from jax.sharding import PartitionSpec as P

MESH = pl.DeviceIdType.MESH
shift_scale = 0.1
tiny_value = 1e-06

ORDER = [
    (0, 0), (3, 0), (1, 0), (0, 3), (0, 1), (2, 0), (3, 3), (3, 1),
    (1, 3), (1, 1), (0, 2), (2, 3), (2, 1), (3, 2), (1, 2), (2, 2),
]
SLOT = {home: k for k, home in enumerate(ORDER)}
ROWS = {(0, 0): (0, 512), (0, 1): (512, 512), (1, 0): (1024, 384), (1, 1): (1408, 384)}
UP, UM, VP, VM = 0, 1, 2, 3
NSEND = 68


def table(k, values):
    total = k * 0
    for j, v in enumerate(values):
        if v:
            total = total + (k == j).astype(jnp.int32) * v
    return total


def nt(a, b):
    return lax.dot_general(a, b, (((1,), (1,)), ((), ())), preferred_element_type=jnp.float32)


def tn(a, b, **kw):
    return lax.dot_general(a, b, (((0,), (0,)), ((), ())), preferred_element_type=jnp.float32, **kw)


def kernel(
    tok_h, go_h, gp_h, up_h, dw_h, ip_h, op_h, tm_h,
    y_o, a_o, gram_o, nr_o, sq_o, om_o,
    w_s, g_s, gp_s, up_s, acc_s, m_s, tk_s, ip_s, op_s, tm_s,
    oacc_s, sb_s, pb_s, oa_s, xb_s, xr_s, ap_s, ar_s,
    p32_s, pr_s, cs_s, cr_s, ns_s, nr_s, gram_s,
    lsem, psend, precv, ssem, rsem, sbsend, sbrecv, xsend, xrecv, asend, arecv, tsend, trecv,
):
    d = lax.axis_index("dp")
    t = lax.axis_index("tensor")
    c = lax.rem(d, 2)
    z = lax.rem(lax.div(d, 2), 4)
    y = lax.div(d, 8)
    u = y * (1 - c) + z * c
    v = z * (1 - c) + y * c
    me = d * 4 + t

    def chip(uu, vv):
        return uu * (4 - 3 * c) + vv * (1 + 3 * c)

    def mod4(a):
        return lax.rem(a + 8, 4)

    partner = (d + 1 - 2 * c, t)
    dirs = [
        (chip(mod4(u + 1), v) * 2 + c, t),
        (chip(mod4(u - 1), v) * 2 + c, t),
        (chip(u, mod4(v + 1)) * 2 + c, t),
        (chip(u, mod4(v - 1)) * 2 + c, t),
    ]
    xdev = [None] + [(d, mod4(t + j)) for j in (1, 2, 3)]

    half = pl.multiple_of(c * 1792, 256)
    other = pl.multiple_of((1 - c) * 1792, 256)
    mine = pl.ds(pl.multiple_of(c * 512, 512), 512)
    lanes = pl.ds(pl.multiple_of(c * 128, 128), 128)

    def local(i, src, dst):
        return pltpu.make_async_copy(src, dst, lsem.at[i])

    def locals_(i):
        if i == 0:
            return local(0, dw_h.at[pl.ds(half, 1024)], w_s.at[0, pl.ds(0, 1024), lanes])
        if i == 1:
            return local(1, dw_h.at[pl.ds(half + 1024, 768)], w_s.at[0, pl.ds(1024, 768), lanes])
        src, dst = [
            (go_h, g_s.at[mine]),
            (tok_h, tk_s),
            (ip_h, ip_s),
            (op_h.at[:, pl.ds(half, 1792)], op_s),
            (gp_h.at[:, pl.ds(half, 1792)], gp_s.at[mine]),
            (up_h.at[:, pl.ds(half, 1792)], up_s.at[mine]),
            (tm_h, tm_s),
        ][i - 2]
        return local(i, src, dst)

    for i in range(5):
        locals_(i).start()

    barrier = pltpu.get_barrier_semaphore()
    greeted = [partner] + dirs + xdev[1:]
    for dev in greeted:
        pl.semaphore_signal(barrier, 1, device_id=dev, device_id_type=MESH)
    pl.semaphore_wait(barrier, len(greeted))

    def remote(src, dst, ss, rs, dev):
        return pltpu.make_async_remote_copy(
            src_ref=src, dst_ref=dst, send_sem=ss, recv_sem=rs, device_id=dev, device_id_type=MESH
        )

    def partner_copies(i):
        src, dst = [
            lambda: (dw_h.at[pl.ds(other, 1024)], w_s.at[0, pl.ds(0, 1024), lanes]),
            lambda: (dw_h.at[pl.ds(other + 1024, 768)], w_s.at[0, pl.ds(1024, 768), lanes]),
            lambda: (go_h, g_s.at[mine]),
            lambda: (gp_h.at[:, pl.ds(other, 1792)], gp_s.at[mine]),
            lambda: (up_h.at[:, pl.ds(other, 1792)], up_s.at[mine]),
        ][i]()
        return remote(src, dst, psend.at[i], precv.at[i], partner)

    partner_copies(0).start()
    partner_copies(1).start()
    partner_copies(2).start()

    sends = []

    def send(dirn, src, dst, w, h):
        r0, rn = ROWS[(w, h)]
        rows = pl.ds(r0, rn)
        remote(
            w_s.at[SLOT[src], rows], w_s.at[SLOT[dst], rows],
            ssem.at[len(sends)], rsem.at[SLOT[dst], 2 * w + h], dirs[dirn],
        ).start()
        sends.append((r0, rn))

    def start_own(mine_first):
        which = c if mine_first else 1 - c
        there = pl.ds(pl.multiple_of(which * 128, 128), 128)
        for k in range(2):
            for dirn, dst, h in ((UP, (3, 0), k), (UM, (1, 0), 1 - k), (VP, (0, 3), k), (VM, (0, 1), 1 - k)):
                r0, rn = ROWS[(0, h)]
                rows = pl.ds(r0, rn)
                src = dw_h.at[pl.ds(half + r0, rn)] if mine_first else w_s.at[0, rows, there]
                remote(
                    src, w_s.at[SLOT[dst], rows, there],
                    ssem.at[len(sends)], rsem.at[SLOT[dst], h], dirs[dirn],
                ).start()
                sends.append((r0, rn // 2))

    def landed(home, w, h):
        r0, rn = ROWS[(w, h)]
        ref = w_s.at[SLOT[home], pl.ds(r0, rn)]
        remote(ref, ref, ssem.at[0], rsem.at[SLOT[home], 2 * w + h], dirs[0]).wait_recv()

    def event(home, w, h):
        du, dv = home
        landed(home, w, h)
        if dv == 0:
            if du == 3 and h == 0:
                send(UP, home, (2, 0), w, h)
            if du == 1 and h == 1:
                send(UM, home, (2, 0), w, h)
            send(VP, home, (du, 3), w, h)
            send(VM, home, (du, 1), w, h)
        elif dv == 3 and h == 0:
            send(VP, home, (du, 2), w, h)
        elif dv == 1 and h == 1:
            send(VM, home, (du, 2), w, h)

    def own_u(w):
        for k in range(2):
            send(UP, (0, 0), (3, 0), w, k)
            send(UM, (0, 0), (1, 0), w, 1 - k)

    def own_v(w):
        for k in range(2):
            send(VP, (0, 0), (0, 3), w, k)
            send(VM, (0, 0), (0, 1), w, 1 - k)

    start_own(True)
    partner_copies(0).wait_recv()
    start_own(False)
    locals_(0).wait()
    for i in range(5, 9):
        locals_(i).start()
    partner_copies(3).start()
    partner_copies(4).start()

    for n in range(7):
        acc_s[n] = jnp.zeros((1024, 256), jnp.float32)
    locals_(3).wait()
    locals_(4).wait()

    def act_part(j, carry):
        k = mod4(t + j)
        ap_s[j] = nt(tk_s[pl.ds(pl.multiple_of(k * 128, 128), 128), :], ip_s[...])
        return carry

    lax.fori_loop(0, 4, act_part, 0)

    def act_copies(j):
        return remote(ap_s.at[j], ar_s.at[j], asend.at[j], arecv.at[j], xdev[j])

    for j in (2, 1, 3):
        act_copies(j).start()

    def first_events(w):
        event((3, 0), w, 0)
        event((1, 0), w, 1)
        event((3, 0), w, 1)
        event((1, 0), w, 0)

    def pair_events(du, w):
        event((du, 3), w, 0)
        event((du, 1), w, 1)
        event((du, 3), w, 1)
        event((du, 1), w, 0)

    def both(home, w):
        event(home, w, 0)
        event(home, w, 1)

    first_events(0)
    locals_(2).wait()
    partner_copies(2).wait_recv()

    def gate(rows, n):
        cols = pl.ds(n * 256, 256)
        g = gp_s[rows, cols].astype(jnp.float32)
        s = 1.0 / (1.0 + jnp.exp(-g))
        return up_s[rows, cols].astype(jnp.float32) * s * (1.0 + g * (1.0 - s))

    def gate_tile(i):
        rows = pl.ds(pl.multiple_of(i * 128, 128), 128)
        total = jnp.zeros((128, 128), jnp.float32)
        for n in range(4):
            gg = (acc_s[n, rows, :] * gate(rows, n)).astype(jnp.bfloat16)
            total = total + nt(gg, op_s[:, n * 256 : (n + 1) * 256])
        oacc_s[i] = total

    def gate_ahead_tile(i):
        rows = pl.ds(pl.multiple_of(i * 128, 128), 128)
        for n in range(3):
            m_s[rows, n * 256 : (n + 1) * 256] = gate(rows, n + 4)

    def gram_part(i):
        x = tm_s[pl.ds(pl.multiple_of(i * 2048, 2048), 2048), :]
        gram_s[...] += tn(x, x)

    def at(step):
        w, k = divmod(step, 16)
        if k == 0 and w == 1:
            pass
        if k == 3:
            pair_events(0, w)
        if k == 5:
            both((2, 0), w)
            if w == 0:
                locals_(1).wait()
                partner_copies(1).wait_recv()
                own_u(1)
        if k == 6:
            pair_events(3, w)
        if k == 8:
            pair_events(1, w)
        if k == 10:
            pair_events(2, w)
            if w == 0:
                own_v(1)
            both((0, 2), w)
        if k == 13:
            both((3, 2), w)
            if w == 0:
                first_events(1)
        if k == 14:
            both((1, 2), w)
        if k == 15:
            both((2, 2), w)
        if step == 1:
            for i in range(5, 9):
                locals_(i).wait()
            partner_copies(3).wait_recv()
            partner_copies(4).wait_recv()
            gram_s[...] = jnp.zeros((128, 128), jnp.float32)

    def step_body(e, carry):
        for step in range(32):
            if step in (1, 3, 5, 6, 8, 10, 13, 14, 15, 19, 20, 21, 22, 23, 24, 25, 26, 29, 30, 31):
                pl.when(e == step)(functools.partial(at, step))
        @pl.when((e >= 2) & (e < 10))
        def _():
            gram_part(e - 2)
            gate_ahead_tile(e - 2)

        @pl.when((e >= 17) & (e < 25))
        def _():
            gate_tile(e - 17)

        w = lax.div(e, 16)
        k = lax.rem(e, 16)
        du = table(k, [h[0] for h in ORDER])
        dv = table(k, [h[1] for h in ORDER])
        q = chip(lax.rem(u + du, 4), lax.rem(v + dv, 4))
        cols = pl.ds(pl.multiple_of(q * 256, 256), 256)

        def part(n, carry):
            m = w * 4 + n
            b = w_s[k, pl.ds(pl.multiple_of(m * 256, 256), 256), :]
            acc_s[m] += nt(g_s[:, cols], b)
            return carry

        lax.fori_loop(0, 4 - w, part, 0)
        return carry

    lax.fori_loop(0, 32, step_body, 0)

    def pb_copy(j):
        return remote(sb_s.at[j], pb_s.at[j], sbsend.at[j], sbrecv.at[j], partner)

    def x_copies(j):
        return remote(xb_s.at[j], xr_s.at[j], xsend.at[j], xrecv.at[j], xdev[j])

    def combine(j):
        pb_copy(j).wait_recv()
        xb_s[j] = oa_s[j] + pb_s[j]
        if j:
            x_copies(j).start()

    def tail(i, carry):
        j = table(lax.div(i, 2), [2, 1, 3, 0])
        own = lax.rem(i, 2)
        core = own * c + (1 - own) * (1 - c)
        k = core * 4 + lax.rem(t + j, 4)
        rows = pl.ds(pl.multiple_of(k * 128, 128), 128)
        total = oacc_s[k]
        for n in range(3):
            gg = (acc_s[n + 4, rows, :] * m_s[rows, n * 256 : (n + 1) * 256]).astype(jnp.bfloat16)
            total = total + nt(gg, op_s[:, (n + 4) * 256 : (n + 5) * 256])

        @pl.when(own == 0)
        def _():
            sb_s[j] = total
            pb_copy(j).start()

        @pl.when(own == 1)
        def _():
            oa_s[j] = total

        for step, jj in ((3, 2), (5, 1), (7, 3)):
            pl.when(i == step)(functools.partial(combine, jj))
        return carry

    lax.fori_loop(0, 8, tail, 0)
    combine(0)
    for j in (1, 2, 3):
        act_copies(j).wait_recv()
    act = (ap_s[0] + ar_s[1] + ar_s[2] + ar_s[3]).astype(jnp.bfloat16)
    for j in (1, 2, 3):
        x_copies(j).wait_recv()
    out = (xb_s[0] + xr_s[1] + xr_s[2] + xr_s[3]).astype(jnp.bfloat16)

    proj = tn(act, out).astype(jnp.bfloat16).astype(jnp.float32)
    p32_s[...] = proj[:, None, :]

    def everyone(copy_to):
        def body(r, carry):
            k = lax.rem(me + r, 128)
            copy_to(k, (lax.div(k, 4), lax.rem(k, 4))).start()
            return carry

        lax.fori_loop(1, 128, body, 0, unroll=4)

    everyone(lambda k, dev: remote(p32_s.at[k], pr_s.at[me], tsend.at[0], trecv.at[0], dev))
    pr_s[me] = p32_s[me]

    across = tn(out, act).astype(jnp.bfloat16).astype(jnp.float32)
    totals = [jnp.zeros((8, 128), jnp.float32) for _ in range(8)]
    for i in range(128):
        column = jnp.broadcast_to(across[:, i : i + 1], (128, 128))
        product = column * tm_s[i * 128 : (i + 1) * 128, :].astype(jnp.float32)
        for b in range(16):
            totals[b % 8] = totals[b % 8] + product[8 * b : 8 * b + 8, :]
    total = ((totals[0] + totals[1]) + (totals[2] + totals[3])) + ((totals[4] + totals[5]) + (totals[6] + totals[7]))
    coeff = jnp.sum(total, axis=0, keepdims=True)
    cs_s[...] = coeff
    everyone(lambda k, dev: remote(cs_s, cr_s.at[me], tsend.at[1], trecv.at[1], dev))
    cr_s[me] = coeff
    om_o[...] = tm_s[pl.ds(pl.multiple_of(me * 128, 128), 128), :].astype(jnp.float32)

    def drain(i, ref):
        return remote(ref.at[pl.ds(0, 127)], ref.at[pl.ds(0, 127)], tsend.at[i], trecv.at[i], partner)

    drain(0, pr_s).wait_recv()
    drain(1, cr_s).wait_recv()
    wide = cr_s[:, 0, :]
    narrow = wide.astype(jnp.bfloat16)
    sketch = tn(pr_s[:, 0, :].astype(jnp.bfloat16), narrow)
    squares = jnp.sum(sketch * sketch, axis=0, keepdims=True)
    ns_s[...] = squares
    everyone(lambda k, dev: remote(ns_s, nr_s.at[me], tsend.at[2], trecv.at[2], dev))
    nr_s[me] = squares
    y_o[...] = sketch
    core = tn(wide, narrow.astype(jnp.float32), precision=lax.Precision.HIGHEST)
    a_o[...] = 0.5 * (core + core.T)
    gram_all = gram_s[...]
    gram_o[...] = 0.5 * (gram_all + gram_all.T)
    eye = lax.broadcasted_iota(jnp.int32, (128, 128), 0) == lax.broadcasted_iota(jnp.int32, (128, 128), 1)
    sq_o[...] = jnp.sum(jnp.where(eye, gram_all, 0.0), axis=0, keepdims=True)

    for i, (r0, rn) in enumerate(sends):
        ref = w_s.at[0, pl.ds(r0, rn)]
        remote(ref, ref, ssem.at[i], rsem.at[0, 0], dirs[0]).wait_send()
    for i in range(5):
        partner_copies(i).wait_send()
    for j in (1, 2, 3):
        act_copies(j).wait_send()
        x_copies(j).wait_send()
    for j in range(4):
        pb_copy(j).wait_send()
    drain(0, pr_s).wait_send()
    drain(1, cr_s).wait_send()
    drain(2, nr_s).wait_recv()
    drain(2, nr_s).wait_send()
    nr_o[...] = jnp.sum(nr_s[:, 0, :], axis=0, keepdims=True)


def eliminate(groups):
    groups = list(groups)
    lane = lax.broadcasted_iota(jnp.int32, (8, 128), 1)
    sub = lax.broadcasted_iota(jnp.int32, (8, 128), 0)

    def wide(x):
        return jnp.broadcast_to(x, (8, 128))

    for g in range(16):
        k0 = 8 * g
        inside = (lane >= k0) & (lane < k0 + 8)
        block = groups[g]
        columns = [wide(block[:, k0 + b : k0 + b + 1]) for b in range(8)]
        low = [[wide(columns[b][a : a + 1, :]) if b >= a else None for b in range(8)] for a in range(8)]
        mult = [[None] * 8 for _ in range(8)]
        inv = []
        for a in range(8):
            inv.append(1.0 / low[a][a])
            for b in range(a + 1, 8):
                mult[b][a] = low[a][b] * inv[a]
            for b in range(a + 1, 8):
                for e in range(b, 8):
                    low[b][e] = low[b][e] - mult[b][a] * low[a][e]
        rows = []
        for a in range(8):
            x = jnp.where(inside, jnp.where(lane == k0 + a, 1.0, 0.0), wide(block[a : a + 1, :]))
            for b in range(a):
                x = x - mult[a][b] * rows[b]
            rows.append(x)
        done = block
        for a in range(8):
            done = jnp.where(sub == a, rows[a] * lax.rsqrt(low[a][a]), done)
        groups[g] = done
        for h in range(g + 1, 16):
            below = groups[h]
            solved = []
            for a in range(8):
                x = wide(below[:, k0 + a : k0 + a + 1])
                for b in range(a):
                    x = x - mult[a][b] * solved[b]
                solved.append(x)
            x = jnp.where(inside, 0.0, below)
            for a in range(8):
                x = x - (solved[a] * inv[a]) * rows[a]
            groups[h] = x
    return groups


def finish(y_ref, core_ref, gram_ref, nr_ref, sq_ref, om_ref, out_ref):
    square_sum = jnp.sum(nr_ref[...], axis=1, keepdims=True)
    omega_sq = jnp.sum(sq_ref[...], axis=1, keepdims=True)
    shift = shift_scale * jnp.sqrt(square_sum / (omega_sq + tiny_value))
    core = core_ref[...] + shift * gram_ref[...]
    inverse = jnp.concatenate(eliminate([core[8 * g : 8 * g + 8, :] for g in range(16)]), axis=0)
    under = lax.broadcasted_iota(jnp.int32, (128, 128), 1) <= lax.broadcasted_iota(jnp.int32, (128, 128), 0)
    inverse = jnp.where(under, inverse, 0.0)
    shifted = y_ref[...] + shift * om_ref[...]
    out_ref[...] = lax.dot_general(
        shifted, inverse, (((1,), (1,)), ((), ())),
        precision=lax.Precision.HIGHEST, preferred_element_type=jnp.float32,
    )


def local(tokens, grad_out, gate_pre, up_value, down_weight, in_proj, out_proj, test_matrix):
    f32, bf16 = jnp.float32, jnp.bfloat16
    square = jax.ShapeDtypeStruct((128, 128), f32)
    vmem = pltpu.VMEM
    dma = pltpu.SemaphoreType.DMA
    row = jax.ShapeDtypeStruct((1, 128), f32)
    sketch, core_sketch, gram, squares, omega_sq, omega_own = pl.pallas_call(
        kernel,
        out_shape=(square, square, square, row, row, square),
        in_specs=[pl.BlockSpec(memory_space=pl.ANY)] * 8,
        out_specs=(pl.BlockSpec(memory_space=vmem),) * 6,
        scratch_shapes=[
            vmem((16, 1792, 256), bf16), vmem((1024, 4096), bf16), vmem((1024, 1792), bf16), vmem((1024, 1792), bf16),
            vmem((7, 1024, 256), f32), vmem((1024, 768), f32), vmem((512, 1024), bf16), vmem((128, 1024), bf16),
            vmem((128, 1792), bf16), vmem((16384, 128), bf16),
            vmem((8, 128, 128), f32), vmem((4, 128, 128), f32), vmem((4, 128, 128), f32), vmem((4, 128, 128), f32),
            vmem((4, 128, 128), f32), vmem((4, 128, 128), f32), vmem((4, 128, 128), f32), vmem((4, 128, 128), f32),
            vmem((128, 1, 128), f32), vmem((128, 1, 128), f32), vmem((1, 128), f32), vmem((128, 1, 128), f32),
            vmem((1, 128), f32), vmem((128, 1, 128), f32), vmem((128, 128), f32),
            dma((9,)), dma((5,)), dma((5,)), dma((NSEND,)), dma((16, 4)), dma((4,)), dma((4,)), dma((4,)), dma((4,)),
            dma((4,)), dma((4,)), dma((3,)), dma((3,)),
        ],
        compiler_params=pltpu.CompilerParams(
            collective_id=1, has_side_effects=True, vmem_limit_bytes=60 * 1024 * 1024
        ),
        name="gather_project_sketch",
    )(tokens, grad_out, gate_pre, up_value, down_weight, in_proj, out_proj, test_matrix)
    return pl.pallas_call(
        finish,
        out_shape=square,
        in_specs=[pl.BlockSpec(memory_space=vmem)] * 6,
        out_specs=pl.BlockSpec(memory_space=vmem),
        name="factor",
    )(sketch, core_sketch, gram, squares, omega_sq, omega_own)


def solution(mesh):
    in_specs = (
        P("dp", "tensor"),
        P("dp", None),
        P("dp", "tensor"),
        P("dp", "tensor"),
        P("tensor", "dp"),
        P(None, "tensor"),
        P(None, "tensor"),
        P(),
    )
    out_specs = P(("dp", "tensor"), None)
    return jax.shard_map(local, mesh=mesh, in_specs=in_specs, out_specs=out_specs, check_vma=False)
```

```python
import functools

import jax
import jax.numpy as jnp
from jax import lax
from jax.experimental import pallas as pl
from jax.experimental.pallas import tpu as pltpu
from jax.sharding import PartitionSpec as P

MESH = pl.DeviceIdType.MESH
shift_scale = 0.1
tiny_value = 1e-06

ORDER = [
    (0, 0), (3, 0), (1, 0), (0, 3), (0, 1), (2, 0), (3, 3), (3, 1),
    (1, 3), (1, 1), (0, 2), (2, 3), (2, 1), (3, 2), (1, 2), (2, 2),
]
SLOT = {home: k for k, home in enumerate(ORDER)}
TILES = [4, 3]
BASE = [sum(TILES[:w]) for w in range(len(TILES))]
LAST = len(TILES) - 1
ROWS = {(w, h): (256 * BASE[w] + 128 * TILES[w] * h, 128 * TILES[w]) for w in range(LAST + 1) for h in range(2)}
FIRST = 256 * TILES[0]
REST = 1792 - FIRST
UP, UM, VP, VM = 0, 1, 2, 3
NSEND = 30 * len(TILES) + 8


def table(k, values):
    total = k * 0
    for j, v in enumerate(values):
        if v:
            total = total + (k == j).astype(jnp.int32) * v
    return total


def packed(k, values):
    code = [sum(v << (2 * j) for j, v in enumerate(values[i : i + 8])) for i in (0, 8)]
    upper = (k >= 8).astype(jnp.int32)
    word = code[0] + upper * (code[1] - code[0])
    return lax.shift_right_arithmetic(word, 2 * (k - 8 * upper)) & 3


def nt(a, b):
    return lax.dot_general(a, b, (((1,), (1,)), ((), ())), preferred_element_type=jnp.float32)


def tn(a, b, **kw):
    return lax.dot_general(a, b, (((0,), (0,)), ((), ())), preferred_element_type=jnp.float32, **kw)


def kernel(
    tok_h, go_h, gp_h, up_h, dw_h, ip_h, op_h, tm_h,
    y_h, a_h, gram_h, nr_h, sq_h, om_h,
    w_s, g_s, gp_s, up_s, acc_s, m_s, tk_s, ip_s, op_s, tm_s,
    oacc_s, sb_s, pb_s, oa_s, xb_s, xr_s, ap_s, ar_s,
    p32_s, pr_s, ns_s, nr_s, gram_s, y_o, a_o, gram_o, nr_o, sq_o, om_o,
    lsem, psend, precv, ssem, rsem, sbsend, sbrecv, xsend, xrecv, asend, arecv, tsend, trecv, osem,
):
    d = lax.axis_index("dp")
    t = lax.axis_index("tensor")
    c = lax.rem(d, 2)
    z = lax.rem(lax.div(d, 2), 4)
    y = lax.div(d, 8)
    u = y * (1 - c) + z * c
    v = z * (1 - c) + y * c
    me = d * 4 + t

    def chip(uu, vv):
        return uu * (4 - 3 * c) + vv * (1 + 3 * c)

    def mod4(a):
        return lax.rem(a + 8, 4)

    partner = (d + 1 - 2 * c, t)
    dirs = [
        (chip(mod4(u + 1), v) * 2 + c, t),
        (chip(mod4(u - 1), v) * 2 + c, t),
        (chip(u, mod4(v + 1)) * 2 + c, t),
        (chip(u, mod4(v - 1)) * 2 + c, t),
    ]
    xdev = [None] + [(d, mod4(t + j)) for j in (1, 2, 3)]

    half = pl.multiple_of(c * 1792, 256)
    other = pl.multiple_of((1 - c) * 1792, 256)
    mine = pl.ds(pl.multiple_of(c * 512, 512), 512)
    lanes = pl.ds(pl.multiple_of(c * 128, 128), 128)

    def local(i, src, dst):
        return pltpu.make_async_copy(src, dst, lsem.at[i])

    def locals_(i):
        if i == 0:
            return local(0, dw_h.at[pl.ds(half, FIRST)], w_s.at[0, pl.ds(0, FIRST), lanes])
        if i == 1:
            return local(1, dw_h.at[pl.ds(half + FIRST, REST)], w_s.at[0, pl.ds(FIRST, REST), lanes])
        src, dst = [
            (go_h, g_s.at[mine]),
            (tok_h, tk_s),
            (ip_h, ip_s),
            (op_h.at[:, pl.ds(half, 1792)], op_s),
            (gp_h.at[:, pl.ds(half, 1792)], gp_s.at[mine]),
            (up_h.at[:, pl.ds(half, 1792)], up_s.at[mine]),
            (tm_h, tm_s),
        ][i - 2]
        return local(i, src, dst)

    for i in range(5):
        locals_(i).start()

    barrier = pltpu.get_barrier_semaphore()
    greeted = [partner] + dirs + [xdev[1], xdev[3]]
    for dev in greeted:
        pl.semaphore_signal(barrier, 1, device_id=dev, device_id_type=MESH)
    pl.semaphore_wait(barrier, len(greeted))

    def remote(src, dst, ss, rs, dev):
        return pltpu.make_async_remote_copy(
            src_ref=src, dst_ref=dst, send_sem=ss, recv_sem=rs, device_id=dev, device_id_type=MESH
        )

    def partner_copies(i):
        src, dst = [
            lambda: (dw_h.at[pl.ds(other, FIRST)], w_s.at[0, pl.ds(0, FIRST), lanes]),
            lambda: (dw_h.at[pl.ds(other + FIRST, REST)], w_s.at[0, pl.ds(FIRST, REST), lanes]),
            lambda: (go_h, g_s.at[mine]),
            lambda: (gp_h.at[:, pl.ds(other, 1792)], gp_s.at[mine]),
            lambda: (up_h.at[:, pl.ds(other, 1792)], up_s.at[mine]),
        ][i]()
        return remote(src, dst, psend.at[i], precv.at[i], partner)

    partner_copies(0).start()
    partner_copies(1).start()
    partner_copies(2).start()

    sends = []

    def send(dirn, src, dst, w, h):
        r0, rn = ROWS[(w, h)]
        rows = pl.ds(r0, rn)
        remote(
            w_s.at[SLOT[src], rows], w_s.at[SLOT[dst], rows],
            ssem.at[len(sends)], rsem.at[SLOT[dst], 2 * w + h], dirs[dirn],
        ).start()
        sends.append((r0, rn))

    def start_own(mine_first):
        which = c if mine_first else 1 - c
        there = pl.ds(pl.multiple_of(which * 128, 128), 128)
        for k in range(2):
            for dirn, dst, h in ((UP, (3, 0), k), (UM, (1, 0), 1 - k), (VP, (0, 3), k), (VM, (0, 1), 1 - k)):
                r0, rn = ROWS[(0, h)]
                rows = pl.ds(r0, rn)
                src = dw_h.at[pl.ds(half + r0, rn)] if mine_first else w_s.at[0, rows, there]
                remote(
                    src, w_s.at[SLOT[dst], rows, there],
                    ssem.at[len(sends)], rsem.at[SLOT[dst], h], dirs[dirn],
                ).start()
                sends.append((r0, rn // 2))

    def landed(home, w, h):
        r0, rn = ROWS[(w, h)]
        ref = w_s.at[SLOT[home], pl.ds(r0, rn)]
        remote(ref, ref, ssem.at[0], rsem.at[SLOT[home], 2 * w + h], dirs[0]).wait_recv()

    def event(home, w, h):
        du, dv = home
        landed(home, w, h)
        if dv == 0:
            if du == 3 and h == 0:
                send(UP, home, (2, 0), w, h)
            if du == 1 and h == 1:
                send(UM, home, (2, 0), w, h)
            send(VP, home, (du, 3), w, h)
            send(VM, home, (du, 1), w, h)
        elif dv == 3 and h == 0:
            send(VP, home, (du, 2), w, h)
        elif dv == 1 and h == 1:
            send(VM, home, (du, 2), w, h)

    def own_u(w):
        for k in range(2):
            send(UP, (0, 0), (3, 0), w, k)
            send(UM, (0, 0), (1, 0), w, 1 - k)

    def own_v(w):
        for k in range(2):
            send(VP, (0, 0), (0, 3), w, k)
            send(VM, (0, 0), (0, 1), w, 1 - k)

    start_own(True)
    partner_copies(0).wait_recv()
    start_own(False)
    locals_(0).wait()
    for i in range(5, 9):
        locals_(i).start()
    partner_copies(3).start()
    partner_copies(4).start()

    for n in range(7):
        acc_s[n] = jnp.zeros((1024, 256), jnp.float32)
    locals_(3).wait()
    locals_(4).wait()

    def act_part(j, carry):
        k = mod4(t + j)
        ap_s[j] = nt(tk_s[pl.ds(pl.multiple_of(k * 128, 128), 128), :], ip_s[...])
        return carry

    lax.fori_loop(0, 4, act_part, 0)

    def act_copies(j):
        return remote(ap_s.at[j], ar_s.at[j], asend.at[j], arecv.at[j], xdev[j])

    act_copies(1).start()
    act_copies(3).start()

    def first_events(w):
        event((3, 0), w, 0)
        event((1, 0), w, 1)
        event((3, 0), w, 1)
        event((1, 0), w, 0)

    def pair_events(du, w):
        event((du, 3), w, 0)
        event((du, 1), w, 1)
        event((du, 3), w, 1)
        event((du, 1), w, 0)

    def both(home, w):
        event(home, w, 0)
        event(home, w, 1)

    first_events(0)
    locals_(2).wait()
    partner_copies(2).wait_recv()

    def gate(rows, n):
        cols = pl.ds(n * 256, 256)
        g = gp_s[rows, cols].astype(jnp.float32)
        s = 1.0 / (1.0 + jnp.exp(-g))
        return up_s[rows, cols].astype(jnp.float32) * s * (1.0 + g * (1.0 - s))

    def gate_tile(w, i):
        rows = pl.ds(pl.multiple_of(i * 128, 128), 128)
        total = oacc_s[i] if w else jnp.zeros((128, 128), jnp.float32)
        for n in range(BASE[w], BASE[w + 1]):
            gg = (acc_s[n, rows, :] * gate(rows, n)).astype(jnp.bfloat16)
            total = total + nt(gg, op_s[:, n * 256 : (n + 1) * 256])
        oacc_s[i] = total

    def gate_ahead_tile(i):
        rows = pl.ds(pl.multiple_of(i * 128, 128), 128)
        for n in range(TILES[LAST]):
            m_s[rows, n * 256 : (n + 1) * 256] = gate(rows, n + BASE[LAST])

    def gram_part(i):
        x = tm_s[pl.ds(pl.multiple_of(i * 2048, 2048), 2048), :]
        gram_s[...] += tn(x, x)

    def at(step):
        w, k = divmod(step, 16)
        if k == 3:
            pair_events(0, w)
        if k == 5:
            both((2, 0), w)
            if w == 0:
                locals_(1).wait()
                partner_copies(1).wait_recv()
            if w < LAST:
                own_u(w + 1)
        if k == 6:
            pair_events(3, w)
        if k == 8:
            pair_events(1, w)
        if k == 10:
            pair_events(2, w)
            if w < LAST:
                own_v(w + 1)
            both((0, 2), w)
        if k == 13:
            both((3, 2), w)
            if w < LAST:
                first_events(w + 1)
        if k == 14:
            both((1, 2), w)
        if k == 15:
            both((2, 2), w)
        if step == 1:
            for i in range(5, 9):
                locals_(i).wait()
            partner_copies(3).wait_recv()
            partner_copies(4).wait_recv()
            gram_s[...] = jnp.zeros((128, 128), jnp.float32)
            act_copies(1).wait_recv()
            act_copies(2).start()

    def step_body(e, carry):
        def events(group):
            for step in range(8 * group, 8 * group + 8):
                if step == 1 or step % 16 in (3, 5, 6, 8, 10, 13, 14, 15):
                    pl.when(e == step)(functools.partial(at, step))

        for group in range(2 * len(TILES)):
            pl.when(lax.div(e, 8) == group)(functools.partial(events, group))
        @pl.when((e >= 2) & (e < 10))
        def _():
            gram_part(e - 2)
            gate_ahead_tile(e - 2)

        for wave in range(LAST):
            begin = 16 * wave + 17
            pl.when((e >= begin) & (e < begin + 8))(functools.partial(lambda wave, begin: gate_tile(wave, e - begin), wave, begin))

        w = lax.div(e, 16)
        k = lax.rem(e, 16)
        du = packed(k, [h[0] for h in ORDER])
        dv = packed(k, [h[1] for h in ORDER])
        q = chip(lax.rem(u + du, 4), lax.rem(v + dv, 4))
        cols = pl.ds(pl.multiple_of(q * 256, 256), 256)

        def part(n, carry):
            m = table(w, BASE) + n
            b = w_s[k, pl.ds(pl.multiple_of(m * 256, 256), 256), :]
            acc_s[m] += nt(g_s[:, cols], b)
            return carry

        lax.fori_loop(0, table(w, TILES), part, 0)
        return carry

    lax.fori_loop(0, 16 * len(TILES), step_body, 0)

    def pb_copy(j):
        return remote(sb_s.at[j], pb_s.at[j], sbsend.at[j], sbrecv.at[j], partner)

    def x_copies(j):
        return remote(xb_s.at[j], xr_s.at[j], xsend.at[j], xrecv.at[j], xdev[j])

    def combine(j):
        pb_copy(j).wait_recv()
        xb_s[j] = oa_s[j] + pb_s[j]
        if j:
            x_copies(j).start()

    def tail(i, carry):
        j = table(i, [2, 1, 3, 2, 1, 3, 0, 0])
        own = table(i, [0, 0, 0, 1, 1, 1, 0, 1])
        core = own * c + (1 - own) * (1 - c)
        k = core * 4 + lax.rem(t + j, 4)
        rows = pl.ds(pl.multiple_of(k * 128, 128), 128)
        total = oacc_s[k]
        for n in range(TILES[LAST]):
            gg = (acc_s[n + BASE[LAST], rows, :] * m_s[rows, n * 256 : (n + 1) * 256]).astype(jnp.bfloat16)
            total = total + nt(gg, op_s[:, (n + BASE[LAST]) * 256 : (n + BASE[LAST] + 1) * 256])

        @pl.when(own == 0)
        def _():
            sb_s[j] = total
            pb_copy(j).start()

        @pl.when(own == 1)
        def _():
            oa_s[j] = total

        for step, jj in ((3, 2), (4, 1), (5, 3)):
            pl.when(i == step)(functools.partial(combine, jj))
        return carry

    lax.fori_loop(0, 8, tail, 0)
    combine(0)
    for j in (2, 3):
        act_copies(j).wait_recv()
    act = (ap_s[0] + ar_s[1] + ar_s[2] + ar_s[3]).astype(jnp.bfloat16)
    for j in (1, 2, 3):
        x_copies(j).wait_recv()
    out = (xb_s[0] + xr_s[1] + xr_s[2] + xr_s[3]).astype(jnp.bfloat16)

    proj = tn(act, out).astype(jnp.bfloat16).astype(jnp.float32)
    p32_s[:, 0, :] = proj

    def everyone(copy_to):
        def body(r, carry):
            k = lax.rem(me + r, 128)
            copy_to(k, (lax.div(k, 4), lax.rem(k, 4))).start()
            return carry

        lax.fori_loop(1, 128, body, 0, unroll=4)

    across = tn(out, act).astype(jnp.bfloat16).astype(jnp.float32)
    totals = [jnp.zeros((8, 128), jnp.float32) for _ in range(8)]
    for i in range(128):
        column = jnp.broadcast_to(across[:, i : i + 1], (128, 128))
        product = column * tm_s[i * 128 : (i + 1) * 128, :].astype(jnp.float32)
        for b in range(16):
            totals[b % 8] = totals[b % 8] + product[8 * b : 8 * b + 8, :]
    total = ((totals[0] + totals[1]) + (totals[2] + totals[3])) + ((totals[4] + totals[5]) + (totals[6] + totals[7]))
    coeff = jnp.sum(total, axis=0, keepdims=True)
    p32_s[:, 1, :] = jnp.broadcast_to(coeff, (128, 128))
    everyone(lambda k, dev: remote(p32_s.at[k], pr_s.at[me], tsend.at[0], trecv.at[0], dev))
    pr_s[me] = p32_s[me]
    om_o[...] = tm_s[pl.ds(pl.multiple_of(me * 128, 128), 128), :].astype(jnp.float32)

    def drain(i, ref):
        return remote(ref.at[pl.ds(0, 127)], ref.at[pl.ds(0, 127)], tsend.at[i], trecv.at[i], partner)

    drain(0, pr_s).wait_recv()
    wide = pr_s[:, 1, :]
    narrow = wide.astype(jnp.bfloat16)
    sketch = tn(pr_s[:, 0, :].astype(jnp.bfloat16), narrow)
    squares = jnp.sum(sketch * sketch, axis=0, keepdims=True)
    ns_s[...] = squares
    everyone(lambda k, dev: remote(ns_s, nr_s.at[me], tsend.at[1], trecv.at[1], dev))
    nr_s[me] = squares
    y_o[...] = sketch
    core = tn(wide, narrow.astype(jnp.float32), precision=lax.Precision.HIGHEST)
    a_o[...] = 0.5 * (core + core.T)
    gram_all = gram_s[...]
    gram_o[...] = 0.5 * (gram_all + gram_all.T)
    eye = lax.broadcasted_iota(jnp.int32, (128, 128), 0) == lax.broadcasted_iota(jnp.int32, (128, 128), 1)
    sq_o[...] = jnp.sum(jnp.where(eye, gram_all, 0.0), axis=0, keepdims=True)

    def leave(i):
        src, dst = [(y_o, y_h), (a_o, a_h), (gram_o, gram_h), (sq_o, sq_h), (om_o, om_h), (nr_o, nr_h)][i]
        return pltpu.make_async_copy(src, dst, osem.at[i])

    for i in range(5):
        leave(i).start()

    for i, (r0, rn) in enumerate(sends):
        ref = w_s.at[0, pl.ds(r0, rn)]
        remote(ref, ref, ssem.at[i], rsem.at[0, 0], dirs[0]).wait_send()
    for i in range(5):
        partner_copies(i).wait_send()
    for j in (1, 2, 3):
        act_copies(j).wait_send()
        x_copies(j).wait_send()
    for j in range(4):
        pb_copy(j).wait_send()
    drain(0, pr_s).wait_send()
    drain(1, nr_s).wait_recv()
    drain(1, nr_s).wait_send()
    nr_o[...] = jnp.sum(nr_s[:, 0, :], axis=0, keepdims=True)
    leave(5).start()
    for i in range(6):
        leave(i).wait()


def eliminate(groups):
    groups = list(groups)
    lane = lax.broadcasted_iota(jnp.int32, (8, 128), 1)
    sub = lax.broadcasted_iota(jnp.int32, (8, 128), 0)

    def wide(x):
        return jnp.broadcast_to(x, (8, 128))

    for g in range(16):
        k0 = 8 * g
        inside = (lane >= k0) & (lane < k0 + 8)
        block = groups[g]
        columns = [wide(block[:, k0 + b : k0 + b + 1]) for b in range(8)]
        low = [[wide(columns[b][a : a + 1, :]) if b >= a else None for b in range(8)] for a in range(8)]
        mult = [[None] * 8 for _ in range(8)]
        inv = []
        for a in range(8):
            inv.append(1.0 / low[a][a])
            for b in range(a + 1, 8):
                mult[b][a] = low[a][b] * inv[a]
            for b in range(a + 1, 8):
                for e in range(b, 8):
                    low[b][e] = low[b][e] - mult[b][a] * low[a][e]
        rows = []
        for a in range(8):
            x = jnp.where(inside, jnp.where(lane == k0 + a, 1.0, 0.0), wide(block[a : a + 1, :]))
            for b in range(a):
                x = x - mult[a][b] * rows[b]
            rows.append(x)
        scaled = [rows[a] * inv[a] for a in range(8)]
        done = block
        for a in range(8):
            done = jnp.where(sub == a, rows[a] * lax.rsqrt(low[a][a]), done)
        groups[g] = done
        for h in range(g + 1, 16):
            below = groups[h]
            solved = [wide(below[:, k0 + a : k0 + a + 1]) for a in range(8)]
            x = jnp.where(inside, 0.0, below)
            for a in range(8):
                for b in range(a + 1, 8):
                    solved[b] = solved[b] - mult[b][a] * solved[a]
                x = x - solved[a] * scaled[a]
            groups[h] = x
    return groups


def finish(y_ref, core_ref, gram_ref, nr_ref, sq_ref, om_ref, out_ref):
    square_sum = jnp.sum(nr_ref[...], axis=1, keepdims=True)
    omega_sq = jnp.sum(sq_ref[...], axis=1, keepdims=True)
    shift = shift_scale * jnp.sqrt(square_sum / (omega_sq + tiny_value))
    core = core_ref[...] + shift * gram_ref[...]
    inverse = jnp.concatenate(eliminate([core[8 * g : 8 * g + 8, :] for g in range(16)]), axis=0)
    under = lax.broadcasted_iota(jnp.int32, (128, 128), 1) <= lax.broadcasted_iota(jnp.int32, (128, 128), 0)
    inverse = jnp.where(under, inverse, 0.0)
    shifted = y_ref[...] + shift * om_ref[...]
    out_ref[...] = lax.dot_general(
        shifted, inverse, (((1,), (1,)), ((), ())),
        precision=lax.Precision.HIGHEST, preferred_element_type=jnp.float32,
    )


def local(tokens, grad_out, gate_pre, up_value, down_weight, in_proj, out_proj, test_matrix):
    f32, bf16 = jnp.float32, jnp.bfloat16
    square = jax.ShapeDtypeStruct((128, 128), f32)
    vmem = pltpu.VMEM
    dma = pltpu.SemaphoreType.DMA
    row = jax.ShapeDtypeStruct((1, 128), f32)
    sketch, core_sketch, gram, squares, omega_sq, omega_own = pl.pallas_call(
        kernel,
        out_shape=(square, square, square, row, row, square),
        in_specs=[pl.BlockSpec(memory_space=pl.ANY)] * 8,
        out_specs=(pl.BlockSpec(memory_space=pl.ANY),) * 6,
        scratch_shapes=[
            vmem((16, 1792, 256), bf16), vmem((1024, 4096), bf16), vmem((1024, 1792), bf16), vmem((1024, 1792), bf16),
            vmem((7, 1024, 256), f32), vmem((1024, 256 * TILES[LAST]), f32), vmem((512, 1024), bf16), vmem((128, 1024), bf16),
            vmem((128, 1792), bf16), vmem((16384, 128), bf16),
            vmem((8, 128, 128), f32), vmem((4, 128, 128), f32), vmem((4, 128, 128), f32), vmem((4, 128, 128), f32),
            vmem((4, 128, 128), f32), vmem((4, 128, 128), f32), vmem((4, 128, 128), f32), vmem((4, 128, 128), f32),
            vmem((128, 2, 128), f32), vmem((128, 2, 128), f32), vmem((1, 128), f32), vmem((128, 1, 128), f32), vmem((128, 128), f32),
            vmem((128, 128), f32), vmem((128, 128), f32), vmem((128, 128), f32), vmem((1, 128), f32), vmem((1, 128), f32), vmem((128, 128), f32),
            dma((9,)), dma((5,)), dma((5,)), dma((NSEND,)), dma((16, 2 * len(TILES))), dma((4,)), dma((4,)), dma((4,)), dma((4,)),
            dma((4,)), dma((4,)), dma((2,)), dma((2,)), dma((6,)),
        ],
        compiler_params=pltpu.CompilerParams(
            collective_id=1, has_side_effects=True, vmem_limit_bytes=60 * 1024 * 1024
        ),
        name="gather_project_sketch",
    )(tokens, grad_out, gate_pre, up_value, down_weight, in_proj, out_proj, test_matrix)
    return pl.pallas_call(
        finish,
        out_shape=square,
        in_specs=[pl.BlockSpec(memory_space=vmem)] * 6,
        out_specs=pl.BlockSpec(memory_space=vmem),
        name="factor",
    )(sketch, core_sketch, gram, squares, omega_sq, omega_own)


def solution(mesh):
    in_specs = (
        P("dp", "tensor"),
        P("dp", None),
        P("dp", "tensor"),
        P("dp", "tensor"),
        P("tensor", "dp"),
        P(None, "tensor"),
        P(None, "tensor"),
        P(),
    )
    out_specs = P(("dp", "tensor"), None)
    return jax.shard_map(local, mesh=mesh, in_specs=in_specs, out_specs=out_specs, check_vma=False)
```

```python
import functools

import jax
import jax.numpy as jnp
from jax import lax
from jax.experimental import pallas as pl
from jax.experimental.pallas import tpu as pltpu
from jax.sharding import PartitionSpec as P

MESH = pl.DeviceIdType.MESH
shift_scale = 0.1
tiny_value = 1e-06

ORDER = [
    (0, 0), (3, 0), (1, 0), (0, 3), (0, 1), (2, 0), (3, 3), (3, 1),
    (1, 3), (1, 1), (0, 2), (2, 3), (2, 1), (3, 2), (1, 2), (2, 2),
]
SLOT = {home: k for k, home in enumerate(ORDER)}
TILES = [4, 3]
BASE = [sum(TILES[:w]) for w in range(len(TILES))]
LAST = len(TILES) - 1
ROWS = {(w, h): (256 * BASE[w] + 128 * TILES[w] * h, 128 * TILES[w]) for w in range(LAST + 1) for h in range(2)}
FIRST = 256 * TILES[0]
REST = 1792 - FIRST
UP, UM, VP, VM = 0, 1, 2, 3
NSEND = 30 * len(TILES) + 8


def table(k, values):
    total = k * 0
    for j, v in enumerate(values):
        if v:
            total = total + (k == j).astype(jnp.int32) * v
    return total


def packed(k, values):
    code = [sum(v << (2 * j) for j, v in enumerate(values[i : i + 8])) for i in (0, 8)]
    upper = (k >= 8).astype(jnp.int32)
    word = code[0] + upper * (code[1] - code[0])
    return lax.shift_right_arithmetic(word, 2 * (k - 8 * upper)) & 3


def nt(a, b):
    return lax.dot_general(a, b, (((1,), (1,)), ((), ())), preferred_element_type=jnp.float32)


def tn(a, b, **kw):
    return lax.dot_general(a, b, (((0,), (0,)), ((), ())), preferred_element_type=jnp.float32, **kw)


def kernel(
    tok_h, go_h, gp_h, up_h, dw_h, ip_h, op_h, tm_h,
    y_h, a_h, gram_h, nr_h, sq_h, om_h,
    w_s, g_s, gp_s, up_s, acc_s, m_s, tk_s, ip_s, op_s, tm_s,
    oacc_s, sb_s, pb_s, oa_s, xb_s, xr_s, ap_s, ar_s,
    p32_s, pr_s, ns_s, nr_s, gram_s, y_o, a_o, gram_o, nr_o, sq_o, om_o,
    lsem, psend, precv, ssem, rsem, sbsend, sbrecv, xsend, xrecv, asend, arecv, tsend, trecv, osem,
):
    d = lax.axis_index("dp")
    t = lax.axis_index("tensor")
    c = lax.rem(d, 2)
    z = lax.rem(lax.div(d, 2), 4)
    y = lax.div(d, 8)
    u = y * (1 - c) + z * c
    v = z * (1 - c) + y * c
    me = d * 4 + t

    def chip(uu, vv):
        return uu * (4 - 3 * c) + vv * (1 + 3 * c)

    def mod4(a):
        return lax.rem(a + 8, 4)

    partner = (d + 1 - 2 * c, t)
    dirs = [
        (chip(mod4(u + 1), v) * 2 + c, t),
        (chip(mod4(u - 1), v) * 2 + c, t),
        (chip(u, mod4(v + 1)) * 2 + c, t),
        (chip(u, mod4(v - 1)) * 2 + c, t),
    ]
    xdev = [None] + [(d, mod4(t + j)) for j in (1, 2, 3)]

    half = pl.multiple_of(c * 1792, 256)
    other = pl.multiple_of((1 - c) * 1792, 256)
    mine = pl.ds(pl.multiple_of(c * 512, 512), 512)
    lanes = pl.ds(pl.multiple_of(c * 128, 128), 128)

    def local(i, src, dst):
        return pltpu.make_async_copy(src, dst, lsem.at[i])

    def locals_(i):
        if i == 0:
            return local(0, dw_h.at[pl.ds(half, FIRST)], w_s.at[0, pl.ds(0, FIRST), lanes])
        if i == 1:
            return local(1, dw_h.at[pl.ds(half + FIRST, REST)], w_s.at[0, pl.ds(FIRST, REST), lanes])
        src, dst = [
            (go_h, g_s.at[mine]),
            (tok_h, tk_s),
            (ip_h, ip_s),
            (op_h.at[:, pl.ds(half, 1792)], op_s),
            (gp_h.at[:, pl.ds(half, 1792)], gp_s.at[mine]),
            (up_h.at[:, pl.ds(half, 1792)], up_s.at[mine]),
            (tm_h, tm_s),
        ][i - 2]
        return local(i, src, dst)

    for i in range(5):
        locals_(i).start()

    barrier = pltpu.get_barrier_semaphore()
    greeted = [partner] + dirs + [xdev[1], xdev[3]]
    for dev in greeted:
        pl.semaphore_signal(barrier, 1, device_id=dev, device_id_type=MESH)
    pl.semaphore_wait(barrier, len(greeted))

    def remote(src, dst, ss, rs, dev):
        return pltpu.make_async_remote_copy(
            src_ref=src, dst_ref=dst, send_sem=ss, recv_sem=rs, device_id=dev, device_id_type=MESH
        )

    def partner_copies(i):
        src, dst = [
            lambda: (dw_h.at[pl.ds(other, FIRST)], w_s.at[0, pl.ds(0, FIRST), lanes]),
            lambda: (dw_h.at[pl.ds(other + FIRST, REST)], w_s.at[0, pl.ds(FIRST, REST), lanes]),
            lambda: (go_h, g_s.at[mine]),
            lambda: (gp_h.at[:, pl.ds(other, 1792)], gp_s.at[mine]),
            lambda: (up_h.at[:, pl.ds(other, 1792)], up_s.at[mine]),
        ][i]()
        return remote(src, dst, psend.at[i], precv.at[i], partner)

    partner_copies(0).start()
    partner_copies(1).start()
    partner_copies(2).start()

    sends = []

    def send(dirn, src, dst, w, h):
        r0, rn = ROWS[(w, h)]
        rows = pl.ds(r0, rn)
        remote(
            w_s.at[SLOT[src], rows], w_s.at[SLOT[dst], rows],
            ssem.at[len(sends)], rsem.at[SLOT[dst], 2 * w + h], dirs[dirn],
        ).start()
        sends.append((r0, rn))

    def start_own(mine_first):
        which = c if mine_first else 1 - c
        there = pl.ds(pl.multiple_of(which * 128, 128), 128)
        for k in range(2):
            for dirn, dst, h in ((UP, (3, 0), k), (UM, (1, 0), 1 - k), (VP, (0, 3), k), (VM, (0, 1), 1 - k)):
                r0, rn = ROWS[(0, h)]
                rows = pl.ds(r0, rn)
                src = dw_h.at[pl.ds(half + r0, rn)] if mine_first else w_s.at[0, rows, there]
                remote(
                    src, w_s.at[SLOT[dst], rows, there],
                    ssem.at[len(sends)], rsem.at[SLOT[dst], h], dirs[dirn],
                ).start()
                sends.append((r0, rn // 2))

    def landed(home, w, h):
        r0, rn = ROWS[(w, h)]
        ref = w_s.at[SLOT[home], pl.ds(r0, rn)]
        remote(ref, ref, ssem.at[0], rsem.at[SLOT[home], 2 * w + h], dirs[0]).wait_recv()

    def event(home, w, h):
        du, dv = home
        landed(home, w, h)
        if dv == 0:
            if du == 3 and h == 0:
                send(UP, home, (2, 0), w, h)
            if du == 1 and h == 1:
                send(UM, home, (2, 0), w, h)
            send(VP, home, (du, 3), w, h)
            send(VM, home, (du, 1), w, h)
        elif dv == 3 and h == 0:
            send(VP, home, (du, 2), w, h)
        elif dv == 1 and h == 1:
            send(VM, home, (du, 2), w, h)

    def own_u(w):
        for k in range(2):
            send(UP, (0, 0), (3, 0), w, k)
            send(UM, (0, 0), (1, 0), w, 1 - k)

    def own_v(w):
        for k in range(2):
            send(VP, (0, 0), (0, 3), w, k)
            send(VM, (0, 0), (0, 1), w, 1 - k)

    start_own(True)
    partner_copies(0).wait_recv()
    start_own(False)
    locals_(0).wait()
    for i in range(5, 9):
        locals_(i).start()
    partner_copies(3).start()
    partner_copies(4).start()

    for n in range(7):
        acc_s[n] = jnp.zeros((1024, 256), jnp.float32)
    locals_(3).wait()
    locals_(4).wait()

    def act_part(j, carry):
        k = mod4(t + j)
        ap_s[j] = nt(tk_s[pl.ds(pl.multiple_of(k * 128, 128), 128), :], ip_s[...])
        return carry

    lax.fori_loop(0, 4, act_part, 0)

    def act_copies(j):
        return remote(ap_s.at[j], ar_s.at[j], asend.at[j], arecv.at[j], xdev[j])

    act_copies(1).start()
    act_copies(3).start()

    def first_events(w):
        event((3, 0), w, 0)
        event((1, 0), w, 1)
        event((3, 0), w, 1)
        event((1, 0), w, 0)

    def pair_events(du, w):
        event((du, 3), w, 0)
        event((du, 1), w, 1)
        event((du, 3), w, 1)
        event((du, 1), w, 0)

    def both(home, w):
        event(home, w, 0)
        event(home, w, 1)

    first_events(0)
    locals_(2).wait()
    partner_copies(2).wait_recv()

    def gate(rows, n):
        cols = pl.ds(n * 256, 256)
        g = gp_s[rows, cols].astype(jnp.float32)
        s = 1.0 / (1.0 + jnp.exp(-g))
        return up_s[rows, cols].astype(jnp.float32) * s * (1.0 + g * (1.0 - s))

    def gate_tile(w, i):
        rows = pl.ds(pl.multiple_of(i * 128, 128), 128)
        total = oacc_s[i] if w else jnp.zeros((128, 128), jnp.float32)
        for n in range(BASE[w], BASE[w + 1]):
            gg = (acc_s[n, rows, :] * gate(rows, n)).astype(jnp.bfloat16)
            total = total + nt(gg, op_s[:, n * 256 : (n + 1) * 256])
        oacc_s[i] = total

    def gate_ahead_tile(i):
        rows = pl.ds(pl.multiple_of(i * 128, 128), 128)
        for n in range(TILES[LAST]):
            m_s[rows, n * 256 : (n + 1) * 256] = gate(rows, n + BASE[LAST])

    def gram_part(i):
        x = tm_s[pl.ds(pl.multiple_of(i * 2048, 2048), 2048), :]
        gram_s[...] += tn(x, x)

    def at(step):
        w, k = divmod(step, 16)
        if k == 3:
            pair_events(0, w)
        if k == 5:
            both((2, 0), w)
            if w == 0:
                locals_(1).wait()
                partner_copies(1).wait_recv()
            if w < LAST:
                own_u(w + 1)
        if k == 6:
            pair_events(3, w)
        if k == 8:
            pair_events(1, w)
        if k == 10:
            pair_events(2, w)
            if w < LAST:
                own_v(w + 1)
            both((0, 2), w)
        if k == 13:
            both((3, 2), w)
            if w < LAST:
                first_events(w + 1)
        if k == 14:
            both((1, 2), w)
        if k == 15:
            both((2, 2), w)
        if step == 1:
            for i in range(5, 9):
                locals_(i).wait()
            partner_copies(3).wait_recv()
            partner_copies(4).wait_recv()
            gram_s[...] = jnp.zeros((128, 128), jnp.float32)
            act_copies(1).wait_recv()
            act_copies(2).start()

    def step_body(e, carry):
        def events(group):
            for step in range(8 * group, 8 * group + 8):
                if step == 1 or step % 16 in (3, 5, 6, 8, 10, 13, 14, 15):
                    pl.when(e == step)(functools.partial(at, step))

        for group in range(2 * len(TILES)):
            pl.when(lax.div(e, 8) == group)(functools.partial(events, group))
        @pl.when((e >= 2) & (e < 10))
        def _():
            gram_part(e - 2)
            gate_ahead_tile(e - 2)

        for wave in range(LAST):
            begin = 16 * wave + 17
            pl.when((e >= begin) & (e < begin + 8))(functools.partial(lambda wave, begin: gate_tile(wave, e - begin), wave, begin))

        w = lax.div(e, 16)
        k = lax.rem(e, 16)
        du = packed(k, [h[0] for h in ORDER])
        dv = packed(k, [h[1] for h in ORDER])
        q = chip(lax.rem(u + du, 4), lax.rem(v + dv, 4))
        cols = pl.ds(pl.multiple_of(q * 256, 256), 256)

        def part(n, carry):
            m = table(w, BASE) + n
            b = w_s[k, pl.ds(pl.multiple_of(m * 256, 256), 256), :]
            acc_s[m] += nt(g_s[:, cols], b)
            return carry

        lax.fori_loop(0, table(w, TILES), part, 0)
        return carry

    lax.fori_loop(0, 16 * len(TILES), step_body, 0)

    def pb_copy(j):
        return remote(sb_s.at[j], pb_s.at[j], sbsend.at[j], sbrecv.at[j], partner)

    def x_copies(j):
        return remote(xb_s.at[j], xr_s.at[j], xsend.at[j], xrecv.at[j], xdev[j])

    def combine(j):
        pb_copy(j).wait_recv()
        xb_s[j] = oa_s[j] + pb_s[j]
        if j:
            x_copies(j).start()

    def tail(i, carry):
        j = table(i, [2, 1, 3, 2, 1, 3, 0, 0])
        own = table(i, [0, 0, 0, 1, 1, 1, 0, 1])
        core = own * c + (1 - own) * (1 - c)
        k = core * 4 + lax.rem(t + j, 4)
        rows = pl.ds(pl.multiple_of(k * 128, 128), 128)
        total = oacc_s[k]
        for n in range(TILES[LAST]):
            gg = (acc_s[n + BASE[LAST], rows, :] * m_s[rows, n * 256 : (n + 1) * 256]).astype(jnp.bfloat16)
            total = total + nt(gg, op_s[:, (n + BASE[LAST]) * 256 : (n + BASE[LAST] + 1) * 256])

        @pl.when(own == 0)
        def _():
            sb_s[j] = total
            pb_copy(j).start()

        @pl.when(own == 1)
        def _():
            oa_s[j] = total

        for step, jj in ((3, 2), (4, 1), (5, 3)):
            pl.when(i == step)(functools.partial(combine, jj))
        return carry

    lax.fori_loop(0, 8, tail, 0)
    combine(0)
    for j in (2, 3):
        act_copies(j).wait_recv()
    act = (ap_s[0] + ar_s[1] + ar_s[2] + ar_s[3]).astype(jnp.bfloat16)
    for j in (1, 2, 3):
        x_copies(j).wait_recv()
    out = (xb_s[0] + xr_s[1] + xr_s[2] + xr_s[3]).astype(jnp.bfloat16)

    proj = tn(act, out).astype(jnp.bfloat16).astype(jnp.float32)
    p32_s[:, 0, :] = proj

    def everyone(copy_to):
        def body(r, carry):
            k = (me + r) & 127
            copy_to(k, (lax.shift_right_arithmetic(k, 2), k & 3)).start()
            return carry

        lax.fori_loop(1, 128, body, 0, unroll=4)

    across = tn(out, act).astype(jnp.bfloat16).astype(jnp.float32)
    totals = [jnp.zeros((8, 128), jnp.float32) for _ in range(8)]
    parts = [jnp.zeros((1, 128), jnp.float32) for _ in range(4)]
    for i in range(88, 128):
        row = proj[i : i + 1, :].astype(jnp.bfloat16)
        parts[i % 4] = parts[i % 4] + lax.dot_general(
            row, tm_s[i * 128 : (i + 1) * 128, :], (((1,), (0,)), ((), ())), preferred_element_type=jnp.float32
        )
    for i in range(88):
        column = jnp.broadcast_to(across[:, i : i + 1], (128, 128))
        product = column * tm_s[i * 128 : (i + 1) * 128, :].astype(jnp.float32)
        for b in range(16):
            totals[b % 8] = totals[b % 8] + product[8 * b : 8 * b + 8, :]
    total = ((totals[0] + totals[1]) + (totals[2] + totals[3])) + ((totals[4] + totals[5]) + (totals[6] + totals[7]))
    coeff = jnp.sum(total, axis=0, keepdims=True) + ((parts[0] + parts[1]) + (parts[2] + parts[3]))
    p32_s[:, 1, :] = jnp.broadcast_to(coeff, (128, 128))
    everyone(lambda k, dev: remote(p32_s.at[k], pr_s.at[me], tsend.at[0], trecv.at[0], dev))
    pr_s[me] = p32_s[me]
    om_o[...] = tm_s[pl.ds(pl.multiple_of(me * 128, 128), 128), :].astype(jnp.float32)

    def drain(i, ref):
        return remote(ref.at[pl.ds(0, 127)], ref.at[pl.ds(0, 127)], tsend.at[i], trecv.at[i], partner)

    drain(0, pr_s).wait_recv()
    wide = pr_s[:, 1, :]
    narrow = wide.astype(jnp.bfloat16)
    sketch = tn(pr_s[:, 0, :].astype(jnp.bfloat16), narrow)
    squares = jnp.sum(sketch * sketch, axis=0, keepdims=True)
    ns_s[...] = squares
    everyone(lambda k, dev: remote(ns_s, nr_s.at[me], tsend.at[1], trecv.at[1], dev))
    nr_s[me] = squares
    y_o[...] = sketch
    core = tn(wide, narrow.astype(jnp.float32), precision=lax.Precision.HIGHEST)
    a_o[...] = 0.5 * (core + core.T)
    gram_all = gram_s[...]
    gram_o[...] = 0.5 * (gram_all + gram_all.T)
    eye = lax.broadcasted_iota(jnp.int32, (128, 128), 0) == lax.broadcasted_iota(jnp.int32, (128, 128), 1)
    sq_o[...] = jnp.sum(jnp.where(eye, gram_all, 0.0), axis=0, keepdims=True)

    def leave(i):
        src, dst = [(y_o, y_h), (a_o, a_h), (gram_o, gram_h), (sq_o, sq_h), (om_o, om_h), (nr_o, nr_h)][i]
        return pltpu.make_async_copy(src, dst, osem.at[i])

    for i in range(5):
        leave(i).start()

    for i, (r0, rn) in enumerate(sends):
        ref = w_s.at[0, pl.ds(r0, rn)]
        remote(ref, ref, ssem.at[i], rsem.at[0, 0], dirs[0]).wait_send()
    for i in range(5):
        partner_copies(i).wait_send()
    for j in (1, 2, 3):
        act_copies(j).wait_send()
        x_copies(j).wait_send()
    for j in range(4):
        pb_copy(j).wait_send()
    drain(0, pr_s).wait_send()
    drain(1, nr_s).wait_recv()
    drain(1, nr_s).wait_send()
    nr_o[...] = jnp.sum(nr_s[:, 0, :], axis=0, keepdims=True)
    leave(5).start()
    for i in range(6):
        leave(i).wait()


def eliminate(groups):
    groups = list(groups)
    lane = lax.broadcasted_iota(jnp.int32, (8, 128), 1)
    sub = lax.broadcasted_iota(jnp.int32, (8, 128), 0)

    def wide(x):
        return jnp.broadcast_to(x, (8, 128))

    for g in range(16):
        k0 = 8 * g
        inside = (lane >= k0) & (lane < k0 + 8)
        block = groups[g]
        columns = [wide(block[:, k0 + b : k0 + b + 1]) for b in range(8)]
        low = [[wide(columns[b][a : a + 1, :]) if b >= a else None for b in range(8)] for a in range(8)]
        mult = [[None] * 8 for _ in range(8)]
        inv = []
        for a in range(8):
            inv.append(1.0 / low[a][a])
            for b in range(a + 1, 8):
                mult[b][a] = low[a][b] * inv[a]
            for b in range(a + 1, 8):
                for e in range(b, 8):
                    low[b][e] = low[b][e] - mult[b][a] * low[a][e]
        rows = []
        for a in range(8):
            x = jnp.where(inside, jnp.where(lane == k0 + a, 1.0, 0.0), wide(block[a : a + 1, :]))
            for b in range(a):
                x = x - mult[a][b] * rows[b]
            rows.append(x)
        scaled = [rows[a] * inv[a] for a in range(8)]
        done = block
        for a in range(8):
            done = jnp.where(sub == a, rows[a] * lax.rsqrt(low[a][a]), done)
        groups[g] = done
        for h in range(g + 1, 16):
            below = groups[h]
            solved = [wide(below[:, k0 + a : k0 + a + 1]) for a in range(8)]
            x = jnp.where(inside, 0.0, below)
            for a in range(8):
                for b in range(a + 1, 8):
                    solved[b] = solved[b] - mult[b][a] * solved[a]
                x = x - solved[a] * scaled[a]
            groups[h] = x
    return groups


def finish(y_ref, core_ref, gram_ref, nr_ref, sq_ref, om_ref, out_ref):
    square_sum = jnp.sum(nr_ref[...], axis=1, keepdims=True)
    omega_sq = jnp.sum(sq_ref[...], axis=1, keepdims=True)
    shift = shift_scale * jnp.sqrt(square_sum / (omega_sq + tiny_value))
    core = core_ref[...] + shift * gram_ref[...]
    inverse = jnp.concatenate(eliminate([core[8 * g : 8 * g + 8, :] for g in range(16)]), axis=0)
    under = lax.broadcasted_iota(jnp.int32, (128, 128), 1) <= lax.broadcasted_iota(jnp.int32, (128, 128), 0)
    inverse = jnp.where(under, inverse, 0.0)
    shifted = y_ref[...] + shift * om_ref[...]
    out_ref[...] = lax.dot_general(
        shifted, inverse, (((1,), (1,)), ((), ())),
        precision=lax.Precision.HIGHEST, preferred_element_type=jnp.float32,
    )


def local(tokens, grad_out, gate_pre, up_value, down_weight, in_proj, out_proj, test_matrix):
    f32, bf16 = jnp.float32, jnp.bfloat16
    square = jax.ShapeDtypeStruct((128, 128), f32)
    vmem = pltpu.VMEM
    dma = pltpu.SemaphoreType.DMA
    row = jax.ShapeDtypeStruct((1, 128), f32)
    sketch, core_sketch, gram, squares, omega_sq, omega_own = pl.pallas_call(
        kernel,
        out_shape=(square, square, square, row, row, square),
        in_specs=[pl.BlockSpec(memory_space=pl.ANY)] * 8,
        out_specs=(pl.BlockSpec(memory_space=pl.ANY),) * 6,
        scratch_shapes=[
            vmem((16, 1792, 256), bf16), vmem((1024, 4096), bf16), vmem((1024, 1792), bf16), vmem((1024, 1792), bf16),
            vmem((7, 1024, 256), f32), vmem((1024, 256 * TILES[LAST]), f32), vmem((512, 1024), bf16), vmem((128, 1024), bf16),
            vmem((128, 1792), bf16), vmem((16384, 128), bf16),
            vmem((8, 128, 128), f32), vmem((4, 128, 128), f32), vmem((4, 128, 128), f32), vmem((4, 128, 128), f32),
            vmem((4, 128, 128), f32), vmem((4, 128, 128), f32), vmem((4, 128, 128), f32), vmem((4, 128, 128), f32),
            vmem((128, 2, 128), f32), vmem((128, 2, 128), f32), vmem((1, 128), f32), vmem((128, 1, 128), f32), vmem((128, 128), f32),
            vmem((128, 128), f32), vmem((128, 128), f32), vmem((128, 128), f32), vmem((1, 128), f32), vmem((1, 128), f32), vmem((128, 128), f32),
            dma((9,)), dma((5,)), dma((5,)), dma((NSEND,)), dma((16, 2 * len(TILES))), dma((4,)), dma((4,)), dma((4,)), dma((4,)),
            dma((4,)), dma((4,)), dma((2,)), dma((2,)), dma((6,)),
        ],
        compiler_params=pltpu.CompilerParams(
            collective_id=1, has_side_effects=True, vmem_limit_bytes=60 * 1024 * 1024
        ),
        name="gather_project_sketch",
    )(tokens, grad_out, gate_pre, up_value, down_weight, in_proj, out_proj, test_matrix)
    return pl.pallas_call(
        finish,
        out_shape=square,
        in_specs=[pl.BlockSpec(memory_space=vmem)] * 6,
        out_specs=pl.BlockSpec(memory_space=vmem),
        name="factor",
    )(sketch, core_sketch, gram, squares, omega_sq, omega_own)


def solution(mesh):
    in_specs = (
        P("dp", "tensor"),
        P("dp", None),
        P("dp", "tensor"),
        P("dp", "tensor"),
        P("tensor", "dp"),
        P(None, "tensor"),
        P(None, "tensor"),
        P(),
    )
    out_specs = P(("dp", "tensor"), None)
    return jax.shard_map(local, mesh=mesh, in_specs=in_specs, out_specs=out_specs, check_vma=False)
```

```python
import functools

import jax
import jax.numpy as jnp
from jax import lax
from jax.experimental import pallas as pl
from jax.experimental.pallas import tpu as pltpu
from jax.sharding import PartitionSpec as P

MESH = pl.DeviceIdType.MESH
shift_scale = 0.1
tiny_value = 1e-06

ORDER = [
    (0, 0), (3, 0), (1, 0), (0, 3), (0, 1), (2, 0), (3, 3), (3, 1),
    (1, 3), (1, 1), (0, 2), (2, 3), (2, 1), (3, 2), (1, 2), (2, 2),
]
SLOT = {home: k for k, home in enumerate(ORDER)}
TILES = [4, 3]
BASE = [sum(TILES[:w]) for w in range(len(TILES))]
LAST = len(TILES) - 1
ROWS = {(w, h): (256 * BASE[w] + 128 * TILES[w] * h, 128 * TILES[w]) for w in range(LAST + 1) for h in range(2)}
FIRST = 256 * TILES[0]
REST = 1792 - FIRST
UP, UM, VP, VM = 0, 1, 2, 3
NSEND = 30 * len(TILES) + 8


def table(k, values):
    total = k * 0
    for j, v in enumerate(values):
        if v:
            total = total + (k == j).astype(jnp.int32) * v
    return total


def packed(k, values):
    code = [sum(v << (2 * j) for j, v in enumerate(values[i : i + 8])) for i in (0, 8)]
    upper = (k >= 8).astype(jnp.int32)
    word = code[0] + upper * (code[1] - code[0])
    return lax.shift_right_arithmetic(word, 2 * (k - 8 * upper)) & 3


def nt(a, b):
    return lax.dot_general(a, b, (((1,), (1,)), ((), ())), preferred_element_type=jnp.float32)


def tn(a, b, **kw):
    return lax.dot_general(a, b, (((0,), (0,)), ((), ())), preferred_element_type=jnp.float32, **kw)


def kernel(
    tok_h, go_h, gp_h, up_h, dw_h, ip_h, op_h, tm_h,
    y_h, a_h, gram_h, nr_h, sq_h, om_h,
    w_s, g_s, gp_s, up_s, acc_s, m_s, tk_s, ip_s, op_s, tm_s,
    oacc_s, sb_s, pb_s, oa_s, xb_s, xr_s, ap_s, ar_s,
    p32_s, pr_s, ns_s, nr_s, gram_s, y_o, a_o, gram_o, nr_o, sq_o, om_o,
    lsem, psend, precv, ssem, rsem, sbsend, sbrecv, xsend, xrecv, asend, arecv, tsend, trecv, osem,
):
    d = lax.axis_index("dp")
    t = lax.axis_index("tensor")
    c = lax.rem(d, 2)
    z = lax.rem(lax.div(d, 2), 4)
    y = lax.div(d, 8)
    u = y * (1 - c) + z * c
    v = z * (1 - c) + y * c
    me = d * 4 + t

    def chip(uu, vv):
        return uu * (4 - 3 * c) + vv * (1 + 3 * c)

    def mod4(a):
        return lax.rem(a + 8, 4)

    partner = (d + 1 - 2 * c, t)
    dirs = [
        (chip(mod4(u + 1), v) * 2 + c, t),
        (chip(mod4(u - 1), v) * 2 + c, t),
        (chip(u, mod4(v + 1)) * 2 + c, t),
        (chip(u, mod4(v - 1)) * 2 + c, t),
    ]
    xdev = [None] + [(d, mod4(t + j)) for j in (1, 2, 3)]

    half = pl.multiple_of(c * 1792, 256)
    other = pl.multiple_of((1 - c) * 1792, 256)
    mine = pl.ds(pl.multiple_of(c * 512, 512), 512)
    lanes = pl.ds(pl.multiple_of(c * 128, 128), 128)

    def local(i, src, dst):
        return pltpu.make_async_copy(src, dst, lsem.at[i])

    def locals_(i):
        if i == 0:
            return local(0, dw_h.at[pl.ds(half, FIRST)], w_s.at[0, pl.ds(0, FIRST), lanes])
        if i == 1:
            return local(1, dw_h.at[pl.ds(half + FIRST, REST)], w_s.at[0, pl.ds(FIRST, REST), lanes])
        src, dst = [
            (go_h, g_s.at[mine]),
            (tok_h, tk_s),
            (ip_h, ip_s),
            (op_h.at[:, pl.ds(half, 1792)], op_s),
            (gp_h.at[:, pl.ds(half, 1792)], gp_s.at[mine]),
            (up_h.at[:, pl.ds(half, 1792)], up_s.at[mine]),
            (tm_h, tm_s),
        ][i - 2]
        return local(i, src, dst)

    for i in range(5):
        locals_(i).start()

    barrier = pltpu.get_barrier_semaphore()
    greeted = [partner] + dirs + [xdev[1], xdev[3]]
    for dev in greeted:
        pl.semaphore_signal(barrier, 1, device_id=dev, device_id_type=MESH)
    pl.semaphore_wait(barrier, len(greeted))

    def remote(src, dst, ss, rs, dev):
        return pltpu.make_async_remote_copy(
            src_ref=src, dst_ref=dst, send_sem=ss, recv_sem=rs, device_id=dev, device_id_type=MESH
        )

    def partner_copies(i):
        src, dst = [
            lambda: (dw_h.at[pl.ds(other, FIRST)], w_s.at[0, pl.ds(0, FIRST), lanes]),
            lambda: (dw_h.at[pl.ds(other + FIRST, REST)], w_s.at[0, pl.ds(FIRST, REST), lanes]),
            lambda: (go_h, g_s.at[mine]),
            lambda: (gp_h.at[:, pl.ds(other, 1792)], gp_s.at[mine]),
            lambda: (up_h.at[:, pl.ds(other, 1792)], up_s.at[mine]),
        ][i]()
        return remote(src, dst, psend.at[i], precv.at[i], partner)

    partner_copies(0).start()
    partner_copies(1).start()
    partner_copies(2).start()

    sends = []

    def send(dirn, src, dst, w, h):
        r0, rn = ROWS[(w, h)]
        rows = pl.ds(r0, rn)
        remote(
            w_s.at[SLOT[src], rows], w_s.at[SLOT[dst], rows],
            ssem.at[len(sends)], rsem.at[SLOT[dst], 2 * w + h], dirs[dirn],
        ).start()
        sends.append((r0, rn))

    def start_own(mine_first):
        which = c if mine_first else 1 - c
        there = pl.ds(pl.multiple_of(which * 128, 128), 128)
        for k in range(2):
            for dirn, dst, h in ((UP, (3, 0), k), (UM, (1, 0), 1 - k), (VP, (0, 3), k), (VM, (0, 1), 1 - k)):
                r0, rn = ROWS[(0, h)]
                rows = pl.ds(r0, rn)
                src = dw_h.at[pl.ds(half + r0, rn)] if mine_first else w_s.at[0, rows, there]
                remote(
                    src, w_s.at[SLOT[dst], rows, there],
                    ssem.at[len(sends)], rsem.at[SLOT[dst], h], dirs[dirn],
                ).start()
                sends.append((r0, rn // 2))

    def landed(home, w, h):
        r0, rn = ROWS[(w, h)]
        ref = w_s.at[SLOT[home], pl.ds(r0, rn)]
        remote(ref, ref, ssem.at[0], rsem.at[SLOT[home], 2 * w + h], dirs[0]).wait_recv()

    def event(home, w, h):
        du, dv = home
        landed(home, w, h)
        if dv == 0:
            if du == 3 and h == 0:
                send(UP, home, (2, 0), w, h)
            if du == 1 and h == 1:
                send(UM, home, (2, 0), w, h)
            send(VP, home, (du, 3), w, h)
            send(VM, home, (du, 1), w, h)
        elif dv == 3 and h == 0:
            send(VP, home, (du, 2), w, h)
        elif dv == 1 and h == 1:
            send(VM, home, (du, 2), w, h)

    def own_u(w):
        for k in range(2):
            send(UP, (0, 0), (3, 0), w, k)
            send(UM, (0, 0), (1, 0), w, 1 - k)

    def own_v(w):
        for k in range(2):
            send(VP, (0, 0), (0, 3), w, k)
            send(VM, (0, 0), (0, 1), w, 1 - k)

    start_own(True)
    partner_copies(0).wait_recv()
    start_own(False)
    locals_(0).wait()
    for i in range(5, 9):
        locals_(i).start()
    partner_copies(3).start()
    partner_copies(4).start()

    for n in range(7):
        acc_s[n] = jnp.zeros((1024, 256), jnp.float32)
    locals_(3).wait()
    locals_(4).wait()

    def act_part(j, carry):
        k = mod4(t + j)
        ap_s[j] = nt(tk_s[pl.ds(pl.multiple_of(k * 128, 128), 128), :], ip_s[...])
        return carry

    lax.fori_loop(0, 4, act_part, 0)

    def act_copies(j):
        return remote(ap_s.at[j], ar_s.at[j], asend.at[j], arecv.at[j], xdev[j])

    act_copies(1).start()
    act_copies(3).start()

    def first_events(w):
        event((3, 0), w, 0)
        event((1, 0), w, 1)
        event((3, 0), w, 1)
        event((1, 0), w, 0)

    def pair_events(du, w):
        event((du, 3), w, 0)
        event((du, 1), w, 1)
        event((du, 3), w, 1)
        event((du, 1), w, 0)

    def both(home, w):
        event(home, w, 0)
        event(home, w, 1)

    first_events(0)
    locals_(2).wait()
    partner_copies(2).wait_recv()

    def gate(rows, n):
        cols = pl.ds(n * 256, 256)
        g = gp_s[rows, cols].astype(jnp.float32)
        s = 1.0 / (1.0 + jnp.exp(-g))
        return up_s[rows, cols].astype(jnp.float32) * s * (1.0 + g * (1.0 - s))

    def gate_tile(w, i):
        rows = pl.ds(pl.multiple_of(i * 128, 128), 128)
        total = oacc_s[i] if w else jnp.zeros((128, 128), jnp.float32)
        for n in range(BASE[w], BASE[w + 1]):
            gg = (acc_s[n, rows, :] * gate(rows, n)).astype(jnp.bfloat16)
            total = total + nt(gg, op_s[:, n * 256 : (n + 1) * 256])
        oacc_s[i] = total

    def gate_ahead_tile(i):
        rows = pl.ds(pl.multiple_of(i * 128, 128), 128)
        for n in range(TILES[LAST]):
            m_s[rows, n * 256 : (n + 1) * 256] = gate(rows, n + BASE[LAST])

    def gram_part(i):
        x = tm_s[pl.ds(pl.multiple_of(i * 2048, 2048), 2048), :]
        gram_s[...] += tn(x, x)

    def at(step):
        w, k = divmod(step, 16)
        if k == 3:
            pair_events(0, w)
        if k == 5:
            both((2, 0), w)
            if w == 0:
                locals_(1).wait()
                partner_copies(1).wait_recv()
            if w < LAST:
                own_u(w + 1)
        if k == 6:
            pair_events(3, w)
        if k == 8:
            pair_events(1, w)
        if k == 10:
            pair_events(2, w)
            if w < LAST:
                own_v(w + 1)
            both((0, 2), w)
        if k == 13:
            both((3, 2), w)
            if w < LAST:
                first_events(w + 1)
        if k == 14:
            both((1, 2), w)
        if k == 15:
            both((2, 2), w)
        if step == 1:
            for i in range(5, 9):
                locals_(i).wait()
            partner_copies(3).wait_recv()
            partner_copies(4).wait_recv()
            gram_s[...] = jnp.zeros((128, 128), jnp.float32)
            act_copies(1).wait_recv()
            act_copies(2).start()

    def step_body(e, carry):
        def events(group):
            for step in range(8 * group, 8 * group + 8):
                if step == 1 or step % 16 in (3, 5, 6, 8, 10, 13, 14, 15):
                    pl.when(e == step)(functools.partial(at, step))

        for group in range(2 * len(TILES)):
            pl.when(lax.div(e, 8) == group)(functools.partial(events, group))
        @pl.when((e >= 2) & (e < 10))
        def _():
            gram_part(e - 2)
            gate_ahead_tile(e - 2)

        for wave in range(LAST):
            begin = 16 * wave + 17
            pl.when((e >= begin) & (e < begin + 8))(functools.partial(lambda wave, begin: gate_tile(wave, e - begin), wave, begin))

        w = lax.div(e, 16)
        k = lax.rem(e, 16)
        du = packed(k, [h[0] for h in ORDER])
        dv = packed(k, [h[1] for h in ORDER])
        q = chip(lax.rem(u + du, 4), lax.rem(v + dv, 4))
        cols = pl.ds(pl.multiple_of(q * 256, 256), 256)

        def part(n, carry):
            m = table(w, BASE) + n
            b = w_s[k, pl.ds(pl.multiple_of(m * 256, 256), 256), :]
            acc_s[m] += nt(g_s[:, cols], b)
            return carry

        lax.fori_loop(0, table(w, TILES), part, 0)
        return carry

    lax.fori_loop(0, 16 * len(TILES), step_body, 0)

    def pb_copy(j):
        return remote(sb_s.at[j], pb_s.at[j], sbsend.at[j], sbrecv.at[j], partner)

    def x_copies(j):
        return remote(xb_s.at[j], xr_s.at[j], xsend.at[j], xrecv.at[j], xdev[j])

    def combine(j):
        pb_copy(j).wait_recv()
        xb_s[j] = oa_s[j] + pb_s[j]
        if j:
            x_copies(j).start()

    def tail(i, carry):
        j = table(i, [2, 1, 3, 2, 1, 3, 0, 0])
        own = table(i, [0, 0, 0, 1, 1, 1, 0, 1])
        core = own * c + (1 - own) * (1 - c)
        k = core * 4 + lax.rem(t + j, 4)
        rows = pl.ds(pl.multiple_of(k * 128, 128), 128)
        total = oacc_s[k]
        for n in range(TILES[LAST]):
            gg = (acc_s[n + BASE[LAST], rows, :] * m_s[rows, n * 256 : (n + 1) * 256]).astype(jnp.bfloat16)
            total = total + nt(gg, op_s[:, (n + BASE[LAST]) * 256 : (n + BASE[LAST] + 1) * 256])

        @pl.when(own == 0)
        def _():
            sb_s[j] = total
            pb_copy(j).start()

        @pl.when(own == 1)
        def _():
            oa_s[j] = total

        for step, jj in ((3, 2), (4, 1), (5, 3)):
            pl.when(i == step)(functools.partial(combine, jj))
        return carry

    lax.fori_loop(0, 8, tail, 0)
    combine(0)
    for j in (2, 3):
        act_copies(j).wait_recv()
    act = (ap_s[0] + ar_s[1] + ar_s[2] + ar_s[3]).astype(jnp.bfloat16)
    for j in (1, 2, 3):
        x_copies(j).wait_recv()
    out = (xb_s[0] + xr_s[1] + xr_s[2] + xr_s[3]).astype(jnp.bfloat16)

    proj = tn(act, out).astype(jnp.bfloat16).astype(jnp.float32)
    p32_s[:, 0, :] = proj

    def everyone(copy_to):
        def body(r, carry):
            k = (me + r) & 127
            copy_to(k, (lax.shift_right_arithmetic(k, 2), k & 3)).start()
            return carry

        lax.fori_loop(1, 128, body, 0, unroll=4)

    across = tn(out, act).astype(jnp.bfloat16).astype(jnp.float32)
    totals = [jnp.zeros((8, 128), jnp.float32) for _ in range(8)]
    parts = [jnp.zeros((1, 128), jnp.float32) for _ in range(4)]
    for i in range(72, 128):
        row = proj[i : i + 1, :].astype(jnp.bfloat16)
        parts[i % 4] = parts[i % 4] + lax.dot_general(
            row, tm_s[i * 128 : (i + 1) * 128, :], (((1,), (0,)), ((), ())), preferred_element_type=jnp.float32
        )
    for i in range(72):
        column = jnp.broadcast_to(across[:, i : i + 1], (128, 128))
        product = column * tm_s[i * 128 : (i + 1) * 128, :].astype(jnp.float32)
        for b in range(16):
            totals[b % 8] = totals[b % 8] + product[8 * b : 8 * b + 8, :]
    total = ((totals[0] + totals[1]) + (totals[2] + totals[3])) + ((totals[4] + totals[5]) + (totals[6] + totals[7]))
    coeff = jnp.sum(total, axis=0, keepdims=True) + ((parts[0] + parts[1]) + (parts[2] + parts[3]))
    p32_s[:, 1, :] = jnp.broadcast_to(coeff, (128, 128))
    everyone(lambda k, dev: remote(p32_s.at[k], pr_s.at[me], tsend.at[0], trecv.at[0], dev))
    pr_s[me] = p32_s[me]
    om_o[...] = tm_s[pl.ds(pl.multiple_of(me * 128, 128), 128), :].astype(jnp.float32)

    def drain(i, ref):
        return remote(ref.at[pl.ds(0, 127)], ref.at[pl.ds(0, 127)], tsend.at[i], trecv.at[i], partner)

    drain(0, pr_s).wait_recv()
    wide = pr_s[:, 1, :]
    narrow = wide.astype(jnp.bfloat16)
    sketch = tn(pr_s[:, 0, :].astype(jnp.bfloat16), narrow)
    squares = jnp.sum(sketch * sketch, axis=0, keepdims=True)
    ns_s[...] = squares
    everyone(lambda k, dev: remote(ns_s, nr_s.at[me], tsend.at[1], trecv.at[1], dev))
    nr_s[me] = squares
    y_o[...] = sketch
    core = tn(wide, narrow.astype(jnp.float32), precision=lax.Precision.HIGHEST)
    a_o[...] = 0.5 * (core + core.T)
    gram_all = gram_s[...]
    gram_o[...] = 0.5 * (gram_all + gram_all.T)
    eye = lax.broadcasted_iota(jnp.int32, (128, 128), 0) == lax.broadcasted_iota(jnp.int32, (128, 128), 1)
    sq_o[...] = jnp.sum(jnp.where(eye, gram_all, 0.0), axis=0, keepdims=True)

    def leave(i):
        src, dst = [(y_o, y_h), (a_o, a_h), (gram_o, gram_h), (sq_o, sq_h), (om_o, om_h), (nr_o, nr_h)][i]
        return pltpu.make_async_copy(src, dst, osem.at[i])

    for i in range(5):
        leave(i).start()

    for i, (r0, rn) in enumerate(sends):
        ref = w_s.at[0, pl.ds(r0, rn)]
        remote(ref, ref, ssem.at[i], rsem.at[0, 0], dirs[0]).wait_send()
    for i in range(5):
        partner_copies(i).wait_send()
    for j in (1, 2, 3):
        act_copies(j).wait_send()
        x_copies(j).wait_send()
    for j in range(4):
        pb_copy(j).wait_send()
    drain(0, pr_s).wait_send()
    drain(1, nr_s).wait_recv()
    drain(1, nr_s).wait_send()
    nr_o[...] = jnp.sum(nr_s[:, 0, :], axis=0, keepdims=True)
    leave(5).start()
    for i in range(6):
        leave(i).wait()


def eliminate(groups):
    groups = list(groups)
    lane = lax.broadcasted_iota(jnp.int32, (8, 128), 1)
    sub = lax.broadcasted_iota(jnp.int32, (8, 128), 0)

    def wide(x):
        return jnp.broadcast_to(x, (8, 128))

    for g in range(16):
        k0 = 8 * g
        inside = (lane >= k0) & (lane < k0 + 8)
        block = groups[g]
        columns = [wide(block[:, k0 + b : k0 + b + 1]) for b in range(8)]
        low = [[wide(columns[b][a : a + 1, :]) if b >= a else None for b in range(8)] for a in range(8)]
        mult = [[None] * 8 for _ in range(8)]
        inv = []
        for a in range(8):
            inv.append(1.0 / low[a][a])
            for b in range(a + 1, 8):
                mult[b][a] = low[a][b] * inv[a]
            for b in range(a + 1, 8):
                for e in range(b, 8):
                    low[b][e] = low[b][e] - mult[b][a] * low[a][e]
        rows = []
        for a in range(8):
            x = jnp.where(inside, jnp.where(lane == k0 + a, 1.0, 0.0), wide(block[a : a + 1, :]))
            for b in range(a):
                x = x - mult[a][b] * rows[b]
            rows.append(x)
        scaled = [rows[a] * inv[a] for a in range(8)]
        done = block
        for a in range(8):
            done = jnp.where(sub == a, rows[a] * lax.rsqrt(low[a][a]), done)
        groups[g] = done
        for h in range(g + 1, 16):
            below = groups[h]
            solved = [wide(below[:, k0 + a : k0 + a + 1]) for a in range(8)]
            x = jnp.where(inside, 0.0, below)
            for a in range(8):
                for b in range(a + 1, 8):
                    solved[b] = solved[b] - mult[b][a] * solved[a]
                x = x - solved[a] * scaled[a]
            groups[h] = x
    return groups


def finish(y_ref, core_ref, gram_ref, nr_ref, sq_ref, om_ref, out_ref):
    square_sum = jnp.sum(nr_ref[...], axis=1, keepdims=True)
    omega_sq = jnp.sum(sq_ref[...], axis=1, keepdims=True)
    shift = shift_scale * jnp.sqrt(square_sum / (omega_sq + tiny_value))
    core = core_ref[...] + shift * gram_ref[...]
    inverse = jnp.concatenate(eliminate([core[8 * g : 8 * g + 8, :] for g in range(16)]), axis=0)
    under = lax.broadcasted_iota(jnp.int32, (128, 128), 1) <= lax.broadcasted_iota(jnp.int32, (128, 128), 0)
    inverse = jnp.where(under, inverse, 0.0)
    shifted = y_ref[...] + shift * om_ref[...]
    out_ref[...] = lax.dot_general(
        shifted, inverse, (((1,), (1,)), ((), ())),
        precision=lax.Precision.HIGHEST, preferred_element_type=jnp.float32,
    )


def local(tokens, grad_out, gate_pre, up_value, down_weight, in_proj, out_proj, test_matrix):
    f32, bf16 = jnp.float32, jnp.bfloat16
    square = jax.ShapeDtypeStruct((128, 128), f32)
    vmem = pltpu.VMEM
    dma = pltpu.SemaphoreType.DMA
    row = jax.ShapeDtypeStruct((1, 128), f32)
    sketch, core_sketch, gram, squares, omega_sq, omega_own = pl.pallas_call(
        kernel,
        out_shape=(square, square, square, row, row, square),
        in_specs=[pl.BlockSpec(memory_space=pl.ANY)] * 8,
        out_specs=(pl.BlockSpec(memory_space=pl.ANY),) * 6,
        scratch_shapes=[
            vmem((16, 1792, 256), bf16), vmem((1024, 4096), bf16), vmem((1024, 1792), bf16), vmem((1024, 1792), bf16),
            vmem((7, 1024, 256), f32), vmem((1024, 256 * TILES[LAST]), f32), vmem((512, 1024), bf16), vmem((128, 1024), bf16),
            vmem((128, 1792), bf16), vmem((16384, 128), bf16),
            vmem((8, 128, 128), f32), vmem((4, 128, 128), f32), vmem((4, 128, 128), f32), vmem((4, 128, 128), f32),
            vmem((4, 128, 128), f32), vmem((4, 128, 128), f32), vmem((4, 128, 128), f32), vmem((4, 128, 128), f32),
            vmem((128, 2, 128), f32), vmem((128, 2, 128), f32), vmem((1, 128), f32), vmem((128, 1, 128), f32), vmem((128, 128), f32),
            vmem((128, 128), f32), vmem((128, 128), f32), vmem((128, 128), f32), vmem((1, 128), f32), vmem((1, 128), f32), vmem((128, 128), f32),
            dma((9,)), dma((5,)), dma((5,)), dma((NSEND,)), dma((16, 2 * len(TILES))), dma((4,)), dma((4,)), dma((4,)), dma((4,)),
            dma((4,)), dma((4,)), dma((2,)), dma((2,)), dma((6,)),
        ],
        compiler_params=pltpu.CompilerParams(
            collective_id=1, has_side_effects=True, vmem_limit_bytes=60 * 1024 * 1024
        ),
        name="gather_project_sketch",
    )(tokens, grad_out, gate_pre, up_value, down_weight, in_proj, out_proj, test_matrix)
    return pl.pallas_call(
        finish,
        out_shape=square,
        in_specs=[pl.BlockSpec(memory_space=vmem)] * 6,
        out_specs=pl.BlockSpec(memory_space=vmem),
        name="factor",
    )(sketch, core_sketch, gram, squares, omega_sq, omega_own)


def solution(mesh):
    in_specs = (
        P("dp", "tensor"),
        P("dp", None),
        P("dp", "tensor"),
        P("dp", "tensor"),
        P("tensor", "dp"),
        P(None, "tensor"),
        P(None, "tensor"),
        P(),
    )
    out_specs = P(("dp", "tensor"), None)
    return jax.shard_map(local, mesh=mesh, in_specs=in_specs, out_specs=out_specs, check_vma=False)
```
